32 devices in a mesh: state: 8 (over z, y), member: 4 (over x, core).
Axes of the slice: x: 2, y: 2, z: 4, core: 2. Of those that a mesh axis runs over, the one named last changes fastest.
Arguments:
- anomalies: bfloat16 [64, 256, 1024], P('state', 'member'), may hold values from -6 to 6
- tapers: bfloat16 [2, 1024, 1024], replicated, may hold values from 0 to 1, as said below
- nbr_block: int32 [64, 12], P('state'), may hold values from 0 to 63, as said below
- taper_index: int32 [64, 12], P('state'), may hold values from 0 to 1
- pair_count: int32 [64], P('state'), may hold values from 5 to 12, as said below
- obs_cell: int32 [65536], P('state'), may hold values from 0 to 8191, as said below
- obs_value: float32 [65536], P('state'), may hold values from -3 to 3
Outputs:
- increments: float32 [64, 1024], P('state', 'member')
The draws below stay inside these ranges and needn't reach their ends.
Inputs may be any that keep to these rules, and one draw needn't show every extreme that they name: `nbr_block`: every slot of block i names a block whose state index (block // 8) lies within 2 of i // 8 around the closed loop of state indices; slot 0 names i itself, and slots 1 to 4 name blocks at state-index offsets -2 to 2 without 0, in rising order. Block i uses slots 0 to pair_count[i] - 1; at least one block uses all 12 slots. Observation r lies in variable obs_cell[r] of the 8192 variables held by state index r // 8192, counted block by block. `tapers`: Gaspari-Cohn taper values of pairs of variables.
All inputs are finite; a program needn't handle non-finite values.
Results may differ from the reference program's by a relative error of at most 0.0018.
Values may be sent and summed in bfloat16 or wider, within the bound.
A program may use at most 64 MiB of HBM per device.

```python
import jax
import jax.numpy as jnp
from jax import lax

B = 1024
M = 256
HOPS = 2
NEIGHBOUR_SLOTS = 12
KT = 2
BLK_DEV = 8
TOTAL_BLOCKS = 64
OBS_DEV = 8192
NOBS = 65536


def draw_tapers(key, part):
    place_key = jax.random.fold_in(key, 101)
    position = jax.random.uniform(place_key, (B, 2), dtype=jnp.float32)
    offset = 0.15 * jnp.arange(KT).astype(jnp.float32)[:, None, None]
    delta_x = position[None, :, None, 0] - position[None, None, :, 0] + offset
    delta_x = delta_x - jnp.floor(delta_x + 0.5)
    delta_y = position[None, :, None, 1] - position[None, None, :, 1] + 0.0 * offset
    delta_y = delta_y - jnp.floor(delta_y + 0.5)
    scaled = jnp.sqrt(delta_x * delta_x + delta_y * delta_y) / 0.06
    inner = -0.25 * scaled ** 5 + 0.5 * scaled ** 4 + 0.625 * scaled ** 3 - 5.0 / 3.0 * scaled ** 2 + 1.0
    safe = jnp.maximum(scaled, 1.0)
    outer = safe ** 5 / 12.0 - 0.5 * safe ** 4 + 0.625 * safe ** 3 + 5.0 / 3.0 * safe ** 2 - 5.0 * safe + 4.0 - 2.0 / (3.0 * safe)
    taper_value = jnp.where(scaled <= 1.0, inner, jnp.where(scaled <= 2.0, outer, 0.0))
    return jnp.clip(taper_value, 0.0, 1.0).astype(jnp.bfloat16)


def draw_nbr_block(key, part):
    block_numbers = jnp.arange(TOTAL_BLOCKS, dtype=jnp.int32)[:, None]
    home = block_numbers // BLK_DEV
    devices = TOTAL_BLOCKS // BLK_DEV
    fixed_offsets = jnp.concatenate([jnp.zeros((1,), jnp.int32), jnp.arange(-HOPS, 0, dtype=jnp.int32), jnp.arange(1, HOPS + 1, dtype=jnp.int32)])
    fixed_offsets = jnp.broadcast_to(fixed_offsets[None, :], (TOTAL_BLOCKS, 2 * HOPS + 1))
    random_offsets = jax.random.randint(jax.random.fold_in(key, 201), (TOTAL_BLOCKS, NEIGHBOUR_SLOTS - 2 * HOPS - 1), -HOPS, HOPS + 1, dtype=jnp.int32)
    offsets = jnp.concatenate([fixed_offsets, random_offsets], axis=1)
    within = jax.random.randint(jax.random.fold_in(key, 202), (TOTAL_BLOCKS, NEIGHBOUR_SLOTS), 0, BLK_DEV, dtype=jnp.int32)
    slot_ids = jnp.arange(NEIGHBOUR_SLOTS, dtype=jnp.int32)[None, :]
    within = jnp.where(slot_ids == 0, block_numbers % BLK_DEV, within)
    return (home + offsets + devices) % devices * BLK_DEV + within


def draw_pair_count(key, part):
    starting_count = jax.random.randint(jax.random.fold_in(key, 301), (TOTAL_BLOCKS,), 2 * HOPS + 1, 2 * HOPS + 5, dtype=jnp.int32)
    sudden_spike = jax.random.randint(jax.random.fold_in(key, 302), (TOTAL_BLOCKS,), 0, 8, dtype=jnp.int32) == 0
    enforced_flag = jax.random.randint(jax.random.fold_in(key, 303), (), 0, TOTAL_BLOCKS, dtype=jnp.int32)
    block_numbers = jnp.arange(TOTAL_BLOCKS, dtype=jnp.int32)
    return jnp.where(sudden_spike | (block_numbers == enforced_flag), NEIGHBOUR_SLOTS, starting_count).astype(jnp.int32)


def draw_obs_cell(key, part):
    return jax.random.randint(jax.random.fold_in(key, 401), (NOBS,), 0, BLK_DEV * B, dtype=jnp.int32)


def with_ends(array, rng, least, high):
    longest = array.shape.index(max(array.shape))
    spots = []
    for shift in (0, 1):
        where = [jax.random.randint(jax.random.fold_in(rng, axis), (), 0, length) for axis, length in enumerate(array.shape)]
        where[longest] = (where[longest] + shift) % array.shape[longest]
        spots.append(tuple(where))
    return array.at[spots[0]].set(least).at[spots[1]].set(high)


def levels(own_key, extent, split, least, top_value):
    loudness = 1.0
    for dim, blocks in split:
        steps = jax.random.uniform(jax.random.fold_in(jax.random.fold_in(own_key, 6), dim), (blocks,), jnp.float32, least / len(split), top_value / len(split))
        loudness = loudness * jnp.repeat(jnp.exp(steps), extent[dim] // blocks).reshape((-1,) + (1,) * (len(extent) - 1 - dim))
    return loudness


def normal_values(key, dims, width, bound, shards=(), kind=jnp.bfloat16):
    level = levels(key, dims, shards, -0.22, 0.18) if shards else 1.0
    array = jax.random.normal(key, dims, jnp.float32) * width * level
    return jnp.minimum(jnp.maximum(array, -bound), bound).astype(kind)


def setup_inputs(seed: int = 0) -> dict:
    arg_keys = jax.random.split(jax.random.key(seed), 8)
    anomalies = normal_values(arg_keys[0], (TOTAL_BLOCKS, M, B), 1.0, 6.0, ((0, 8), (1, 4)))
    tapers = draw_tapers(jax.random.fold_in(arg_keys[7], 71), 0)
    nbr_block = draw_nbr_block(jax.random.fold_in(arg_keys[7], 71), 0)
    taper_index = with_ends(jax.random.randint(arg_keys[3], (TOTAL_BLOCKS, NEIGHBOUR_SLOTS), 0, KT), jax.random.fold_in(arg_keys[3], 1), 0, KT - 1).astype(jnp.int32)
    pair_count = draw_pair_count(jax.random.fold_in(arg_keys[7], 71), 0)
    obs_cell = draw_obs_cell(jax.random.fold_in(arg_keys[7], 71), 0)
    obs_value = normal_values(arg_keys[6], (NOBS,), 0.5, 3.0, ((0, 8),), jnp.float32)
    return {"anomalies": anomalies, "tapers": tapers, "nbr_block": nbr_block, "taper_index": taper_index, "pair_count": pair_count, "obs_cell": obs_cell, "obs_value": obs_value}


def reference(anomalies, tapers, nbr_block, taper_index, pair_count, obs_cell, obs_value):
    row_ids = jnp.arange(NOBS, dtype=jnp.int32)
    global_cells = (row_ids // OBS_DEV) * (BLK_DEV * B) + obs_cell.astype(jnp.int32)
    observation_residual = jnp.zeros((TOTAL_BLOCKS * B,), jnp.float32).at[global_cells].add(obs_value).reshape(TOTAL_BLOCKS, B)
    weighted_low = (anomalies.astype(jnp.float32) * observation_residual[:, None, :]).astype(jnp.bfloat16)
    weighted_low = lax.optimization_barrier(weighted_low)
    slot_ids = jnp.arange(NEIGHBOUR_SLOTS, dtype=jnp.int32)
    tile_ids = jnp.arange(KT, dtype=jnp.int32)
    taper_wide = tapers.astype(jnp.float32)

    def one_block(block_id):
        is_valid = slot_ids < pair_count[block_id]
        selector = (is_valid[:, None] & (taper_index[block_id][:, None] == tile_ids[None, :])).astype(jnp.float32)
        panels = weighted_low[nbr_block[block_id]].astype(jnp.float32)
        gathered_groups = jnp.einsum('st,smb->tmb', selector, panels,
                             precision=lax.Precision.HIGHEST).astype(jnp.bfloat16)
        gathered_groups = lax.optimization_barrier(gathered_groups).astype(jnp.float32)
        running = jnp.zeros((M, B), jnp.float32)
        for tile_id in range(KT):
            running = running + jnp.dot(gathered_groups[tile_id], taper_wide[tile_id].T,
                                        precision=lax.Precision.HIGHEST)
        member_terms = anomalies[block_id].astype(jnp.float32) * running
        return jnp.sum(member_terms, axis=0) / jnp.float32(M - 1)

    return lax.map(one_block, jnp.arange(TOTAL_BLOCKS, dtype=jnp.int32))
```

```python
import functools

import jax
import jax.numpy as jnp
from jax import lax
from jax.experimental import pallas as pl
from jax.experimental.pallas import tpu as pltpu
from jax.sharding import PartitionSpec as P

M = 256
HOPS = 2
KT = 2
LANES = 128
MC = 16
PIECES = 2
EARLY = 2
MESH = pl.DeviceIdType.MESH


def kernel(
    states, members, slots,
    nbr_hbm, tix_hbm, cnt_hbm, cells_hbm, values_hbm, anom, tapers, out,
    nbr, tix, cnt, near_far, local, tab0, cells, values, obs_s, av, tv, r1, r2, tab_in, idx, innov, innov_in,
    hot, low, z, own_w, wr, v2, acc, part, got,
    tab_s, tab_r, idx_s, av_s, tv_s, s1, q1, s2, q2, in_s, in_r, ps, pr, peers,
):
    blocks, mem, width = anom.shape
    chunks = mem // MC
    last = chunks - 1
    half = blocks // PIECES
    groups = width // LANES
    cols = width // members
    none = KT * 3 * blocks
    d = lax.axis_index("state")
    me = lax.axis_index("member")
    odd = d % 2
    sign = 1 - 2 * odd
    heavy = chunks // 2
    fixed = 2 * HOPS + 1

    def at(ds, dm):
        return ((d + ds + states) % states, (me + dm) % members)

    barrier = pltpu.get_barrier_semaphore()
    greeted = [(sign, 0), (2, 0), (-2, 0)] + [(0, k) for k in range(1, members)]
    for ds, dm in greeted:
        pl.semaphore_signal(barrier, inc=1, device_id=at(ds, dm), device_id_type=MESH)

    load_n = pltpu.make_async_copy(nbr_hbm, nbr, obs_s.at[2])
    load_x = pltpu.make_async_copy(tix_hbm, tix, obs_s.at[3])
    load_p = pltpu.make_async_copy(cnt_hbm, cnt, obs_s.at[4])
    load_a = pltpu.make_async_copy(anom, av, av_s)
    load_t = pltpu.make_async_copy(tapers, tv, tv_s)
    load_c = pltpu.make_async_copy(cells_hbm, cells, obs_s.at[0])
    load_v = pltpu.make_async_copy(values_hbm, values, obs_s.at[1])
    for load in (load_n, load_x, load_p, load_c, load_v, load_a, load_t):
        load.start()

    def remote(src, dst, send, recv, target):
        return pltpu.make_async_remote_copy(
            src_ref=src, dst_ref=dst, send_sem=send, recv_sem=recv,
            device_id=target, device_id_type=MESH,
        )

    def members_of(c, shift):
        return pl.ds(pl.multiple_of(((c + shift * heavy) % chunks) * MC, MC), MC)

    def piece(ref, c, h, shift):
        return ref.at[pl.ds(h * half, half), members_of(c, shift), :]

    def send2(c, h):
        return remote(
            piece(anom, c, h, odd), piece(r2, c, h, 0), s2.at[c, h], q2.at[c, h], at(-2 * sign, 0)
        )

    def send1(c):
        return remote(
            anom.at[:, members_of(c, 1 - odd), :], r1.at[:, members_of(c, 0), :],
            s1.at[c], q1.at[c], at(sign, 0),
        )

    def to(u):
        return sign if u == 1 else -2 * sign

    def send_tab(u):
        return remote(near_far.at[u - 1], tab_in.at[u - 1], tab_s.at[u - 1], tab_r.at[u - 1], at(to(u), 0))

    def send_innov(u):
        return remote(innov, innov_in.at[u - 1], in_s.at[u - 1], in_r.at[u - 1], at(to(u), 0))

    def send_part(u, k):
        return remote(
            part.at[u, (me + k) % members], got.at[u, k], ps.at[u, k], pr.at[u, k],
            at((0, sign, 2 * sign)[u], k),
        )

    order = [(c, h) for c in range(chunks) for h in range(PIECES)]
    pl.semaphore_wait(barrier, len(greeted))
    for c, h in order[:EARLY]:
        send2(c, h).start()
    send1(0).start()
    acc[...] = jnp.zeros_like(acc)

    load_n.wait()
    load_x.wait()
    load_p.wait()
    row = lax.broadcasted_iota(jnp.int32, (blocks, slots), 0)
    slot = lax.broadcasted_iota(jnp.int32, (blocks, slots), 1)
    count = jnp.zeros((blocks, slots), jnp.int32)
    for i in range(blocks):
        count = jnp.where(row == i, cnt[i], count)
    valid = slot < count
    block = nbr[...]
    home = lax.div(block, jnp.int32(blocks))
    base = tix[...] * (3 * blocks) + block - home * blocks
    gap = home - d
    gap = jnp.where(gap > HOPS, gap - states, jnp.where(gap < -HOPS, gap + states, gap)) * sign
    near = jnp.where(gap == 1, base, jnp.where(gap == -1, base + 2 * blocks, none))
    far = jnp.where(gap == -2, base, jnp.where(gap == -1, base + blocks, none))
    near_far[...] = jnp.full(near_far.shape, none, jnp.int32)
    local[...] = jnp.full(local.shape, none, jnp.int32)
    near_far[0, :, 0:slots] = jnp.where(valid, near, none)
    near_far[1, :, 0:slots] = jnp.where(valid, far, none)
    local[0, :, 0:slots] = jnp.where(valid & (gap >= 0), base + gap * blocks, none)
    local[1, :, 0:slots] = jnp.where(valid & (gap == 0), base, none)
    local[2, :, 0:slots] = jnp.where(valid & (gap == 2), base + 2 * blocks, none)
    load_tab = pltpu.make_async_copy(local, tab0, obs_s.at[5])
    load_tab.start()
    for u in (1, 2):
        send_tab(u).start()

    def hot_row(k, carry):
        cell = cells[pl.ds(k, 1), :]
        value = values[pl.ds(k, 1), :]
        lo = cell & (LANES - 1)
        block = cell // width
        group = (cell // LANES) % groups
        hi = group * blocks + block
        v1 = value.astype(jnp.bfloat16).astype(jnp.float32)
        rest = value - v1
        v2 = rest.astype(jnp.bfloat16).astype(jnp.float32)
        v3 = rest - v2
        rows = blocks * groups
        same = lax.broadcasted_iota(jnp.int32, (rows, LANES), 0) == hi
        where = pl.ds(pl.multiple_of(k * LANES, LANES), LANES)
        for n, v in enumerate((v1, v2, v3)):
            hot[pl.ds(n * rows, rows), where] = jnp.where(
                same, jnp.broadcast_to(v, (rows, LANES)), 0.0
            ).astype(jnp.bfloat16)
        low[:, where] = jnp.where(
            lax.broadcasted_iota(jnp.int32, (LANES, LANES), 0) == lo, 1.0, 0.0
        ).astype(jnp.bfloat16)
        return carry

    load_c.wait()
    load_v.wait()
    lax.fori_loop(0, cells.shape[0], hot_row, 0)
    rows = blocks * groups
    sums = lax.dot_general(
        hot[...], low[...], (((1,), (1,)), ((), ())), preferred_element_type=jnp.float32
    )
    total = sums[0:rows] + sums[rows : 2 * rows] + sums[2 * rows : 3 * rows]
    for g in range(groups):
        innov[:, g * LANES : (g + 1) * LANES] = total[g * blocks : (g + 1) * blocks]
    for u in (1, 2):
        send_innov(u).start()
    for c, h in order[EARLY:]:
        send2(c, h).start()
    for c in range(1, heavy):
        send1(c).start()
    for k in range(1, members):
        pl.semaphore_signal(peers, inc=1, device_id=at(0, k), device_id_type=MESH)

    load_a.wait()
    for c in range(chunks):
        for j in range(blocks):
            own_w[c, j] = (
                av[j, members_of(c, odd), :].astype(jnp.float32) * innov[pl.ds(j, 1), :]
            ).astype(jnp.bfloat16)
    load_t.wait()
    nw = width // 2

    def own_z(n, carry):
        t, x = n // 2, n % 2
        where = pl.ds(pl.multiple_of(x * nw, nw), nw)
        res = lax.dot_general(
            own_w[...].reshape(chunks * blocks * MC, width), tv[t, where, :],
            (((1,), (1,)), ((), ())), preferred_element_type=jnp.float32,
        )
        z[:, pl.ds(t * 3 * blocks, blocks), :, where] = res.reshape(chunks, blocks, MC, nw)
        return carry

    lax.fori_loop(0, KT * 2, own_z, 0)
    for c in range(heavy, chunks):
        for t in range(KT):
            z[c, (t * 3 + 1) * blocks : (t * 3 + 2) * blocks] = jnp.zeros((blocks, MC, width), jnp.float32)
    for c in range(chunks):
        z[c, none] = jnp.zeros((MC, width), jnp.float32)

    load_tab.wait()
    for u in (1, 2):
        send_tab(u).wait_recv()
        fill = pltpu.make_async_copy(tab_in.at[u - 1], idx.at[u - 1], idx_s.at[u - 1])
        fill.start()
        fill.wait()

    def offset_slot(g):
        return {-2: 1 + 3 * odd, -1: 2 + odd, 1: 3 - odd, 2: 4 - 3 * odd}[g]

    free = list(range(fixed, slots))

    def spread(c, table, i, named):
        total = z[c, table(i, named[0])]
        for s in named[1:] + free:
            total = total + z[c, table(i, s)]
        return total

    def pairs(c, u, table, named, source, shift):
        def one(i, carry):
            value = source[i, members_of(c, shift), :].astype(jnp.float32) * spread(c, table, i, named)
            acc[u, i] += jnp.sum(value.reshape(MC // 8, 8, width), axis=0)
            return carry

        lax.fori_loop(0, blocks, one, 0)

    def table0(k):
        return lambda i, s: tab0[k, i, s]

    def table_in(u):
        return lambda i, s: idx[u - 1, i, s]

    def fold(u):
        for i in range(blocks):
            line = jnp.sum(acc[u, i], axis=0, keepdims=True)
            for m in range(members):
                part[u, m, i : i + 1, :] = line[:, m * cols : (m + 1) * cols]

    def far_z(c, first):
        for g, r in enumerate((r1, r2)):
            if g or not first:
                for j in range(blocks):
                    wr[g * blocks + j] = (
                        r[j, members_of(c, 0), :].astype(jnp.float32)
                        * innov_in[g, pl.ds(j, 1), :]
                    ).astype(jnp.bfloat16)
        count = 2 * blocks - first

        def one(n, carry):
            t, x = n // 2, n % 2
            where = pl.ds(pl.multiple_of(x * nw, nw), nw)
            res = lax.dot_general(
                wr[pl.ds(first, count)].reshape(count * MC, width), tv[t, where, :],
                (((1,), (1,)), ((), ())), preferred_element_type=jnp.float32,
            )
            z[c, pl.ds(t * 3 * blocks + blocks + first, count), :, where] = res.reshape(
                count, MC, nw
            )
            return carry

        lax.fori_loop(0, KT * 2, one, 0)

    def full_step(c, carry):
        for h in range(PIECES):
            send2(c, h).wait_recv()
        send1(c).wait_recv()
        far_z(c, 0)
        pairs(c, 2, table_in(2), [offset_slot(-2), offset_slot(-1)], r2, 0)
        pairs(c, 1, table_in(1), [offset_slot(-1), offset_slot(1)], r1, 0)
        pairs(c, 0, table0(0), [0, offset_slot(1), offset_slot(2)], av, odd)
        return carry

    for u in (1, 2):
        send_innov(u).wait_recv()
    lax.fori_loop(0, heavy, full_step, 0)
    fold(1)
    pl.semaphore_wait(peers, members - 1)
    for k in range(members):
        send_part(1, k).start()

    def light_step(c, carry):
        for h in range(PIECES):
            send2(c, h).wait_recv()
        far_z(c, blocks)
        pairs(c, 2, table_in(2), [offset_slot(-2)], r2, 0)
        pairs(c, 0, table0(0), [0, offset_slot(2)], av, odd)
        return carry

    lax.fori_loop(heavy, last, light_step, 0)

    def ahead(i, carry):
        v2[i] = spread(last, table_in(2), i, [offset_slot(-2)])
        return carry

    lax.fori_loop(0, blocks, ahead, 0)
    pairs(last, 0, table0(1), [0], av, odd)
    for h in range(PIECES):
        send2(last, h).wait_recv()

    def reach(i, carry):
        value = r2[i, members_of(last, 0), :].astype(jnp.float32) * v2[i]
        acc[2, i] += jnp.sum(value.reshape(MC // 8, 8, width), axis=0)
        return carry

    lax.fori_loop(0, blocks, reach, 0)
    fold(2)
    for k in range(members):
        send_part(2, k).start()
    far_z(last, blocks)
    pairs(last, 0, table0(2), [offset_slot(2)], av, odd)
    fold(0)
    for k in range(1, members):
        send_part(0, k).start()
    total = part[0, me]
    for u in (1, 2, 0):
        for k in range(members):
            if u or k:
                send_part(u, k).wait_recv()
                total = total + got[u, k]
    out[...] = total / jnp.float32(M - 1)

    for u in (1, 2, 0):
        for k in range(members):
            if u or k:
                send_part(u, k).wait_send()
    for u in (1, 2):
        send_tab(u).wait_send()
        send_innov(u).wait_send()
    for c, h in order:
        send2(c, h).wait_send()
    for c in range(heavy):
        send1(c).wait_send()


def on_device(states, members, anomalies, tapers, nbr_block, taper_index, pair_count, obs_cell, obs_value):
    blocks, mem, width = anomalies.shape
    slots = nbr_block.shape[1]
    chunks = mem // MC
    cols = width // members
    cells = obs_cell.reshape(-1, LANES)
    values = obs_value.reshape(-1, LANES)
    rows = blocks * (width // LANES)
    dma = pltpu.SemaphoreType.DMA
    any_space = pl.BlockSpec(memory_space=pl.ANY)
    vmem = pl.BlockSpec(memory_space=pltpu.VMEM)
    return pl.pallas_call(
        functools.partial(kernel, states, members, slots),
        out_shape=pltpu.VMEM((blocks, cols), jnp.float32),
        in_specs=[any_space] * 7,
        out_specs=vmem,
        scratch_shapes=[
            pltpu.VMEM(nbr_block.shape, jnp.int32),
            pltpu.VMEM(taper_index.shape, jnp.int32),
            pltpu.SMEM(pair_count.shape, jnp.int32),
            pltpu.VMEM((2, blocks, LANES), jnp.int32),
            pltpu.VMEM((3, blocks, LANES), jnp.int32),
            pltpu.SMEM((3, blocks, LANES), jnp.int32),
            pltpu.VMEM(cells.shape, jnp.int32),
            pltpu.VMEM(values.shape, jnp.float32),
            dma((6,)),
            pltpu.VMEM((blocks, mem, width), jnp.bfloat16),
            pltpu.VMEM(tapers.shape, jnp.bfloat16),
            pltpu.VMEM((blocks, mem, width), jnp.bfloat16),
            pltpu.VMEM((blocks, mem, width), jnp.bfloat16),
            pltpu.VMEM((2, blocks, LANES), jnp.int32),
            pltpu.SMEM((2, blocks, LANES), jnp.int32),
            pltpu.VMEM((blocks, width), jnp.float32),
            pltpu.VMEM((2, blocks, width), jnp.float32),
            pltpu.VMEM((3 * rows, obs_cell.shape[0]), jnp.bfloat16),
            pltpu.VMEM((LANES, obs_cell.shape[0]), jnp.bfloat16),
            pltpu.VMEM((chunks, KT * 3 * blocks + 1, MC, width), jnp.float32),
            pltpu.VMEM((chunks, blocks, MC, width), jnp.bfloat16),
            pltpu.VMEM((2 * blocks, MC, width), jnp.bfloat16),
            pltpu.VMEM((blocks, MC, width), jnp.float32),
            pltpu.VMEM((3, blocks, 8, width), jnp.float32),
            pltpu.VMEM((3, members, blocks, cols), jnp.float32),
            pltpu.VMEM((3, members, blocks, cols), jnp.float32),
            dma((2,)), dma((2,)), dma((2,)), dma, dma,
            dma((chunks,)), dma((chunks,)),
            dma((chunks, PIECES)), dma((chunks, PIECES)),
            dma((2,)), dma((2,)),
            dma((3, members)), dma((3, members)),
            pltpu.SemaphoreType.REGULAR,
        ],
        compiler_params=pltpu.CompilerParams(
            collective_id=0, has_side_effects=True, vmem_limit_bytes=66_000_000
        ),
    )(nbr_block, taper_index, pair_count, cells, values, anomalies, tapers)


def solution(mesh):
    placed = (
        P("state", "member", None),
        P(),
        P("state", None),
        P("state", None),
        P("state"),
        P("state"),
        P("state"),
    )
    return jax.shard_map(
        functools.partial(on_device, mesh.shape["state"], mesh.shape["member"]),
        mesh=mesh, in_specs=placed, out_specs=P("state", "member"), check_vma=False,
    )
```

```python
import functools

import jax
import jax.numpy as jnp
from jax import lax
from jax.experimental import pallas as pl
from jax.experimental.pallas import tpu as pltpu
from jax.sharding import PartitionSpec as P

M = 256
HOPS = 2
KT = 2
LANES = 128
MC = 16
MESH = pl.DeviceIdType.MESH


def kernel(
    states, members, slots,
    nbr_hbm, tix_hbm, cnt_hbm, cells_hbm, values_hbm, anom, tapers, out,
    nbr, tix, cnt, near_far, local, tab0, cells, values, obs_s, av, tv, r1, r2, tab_in, idx, innov, innov_in,
    hot, low, z, own_w, wr, v2, acc, part, got,
    tab_s, tab_r, idx_s, av_s, tv_s, s1, q1, s2, q2, s3, q3, in_s, in_r, fs, fr, ps, pr, peers,
):
    blocks, mem, width = anom.shape
    chunks = mem // MC
    last = chunks - 1
    groups = width // LANES
    cols = width // members
    none = KT * 3 * blocks
    d = lax.axis_index("state")
    me = lax.axis_index("member")
    odd = d % 2
    sign = 1 - 2 * odd
    heavy = chunks // 2
    fixed = 2 * HOPS + 1

    def at(ds, dm):
        return ((d + ds + states) % states, (me + dm) % members)

    barrier = pltpu.get_barrier_semaphore()
    greeted = [(sign, 0), (2, 0), (-2, 0)] + [(0, k) for k in range(1, members)]
    for ds, dm in greeted:
        pl.semaphore_signal(barrier, inc=1, device_id=at(ds, dm), device_id_type=MESH)

    load_n = pltpu.make_async_copy(nbr_hbm, nbr, obs_s.at[2])
    load_x = pltpu.make_async_copy(tix_hbm, tix, obs_s.at[3])
    load_p = pltpu.make_async_copy(cnt_hbm, cnt, obs_s.at[4])
    load_a = pltpu.make_async_copy(anom, av, av_s)
    load_t = pltpu.make_async_copy(tapers, tv, tv_s)
    load_c = pltpu.make_async_copy(cells_hbm, cells, obs_s.at[0])
    load_v = pltpu.make_async_copy(values_hbm, values, obs_s.at[1])

    def remote(src, dst, send, recv, target):
        return pltpu.make_async_remote_copy(
            src_ref=src, dst_ref=dst, send_sem=send, recv_sem=recv,
            device_id=target, device_id_type=MESH,
        )

    def members_of(c, shift):
        return pl.ds(pl.multiple_of(((c + shift * heavy) % chunks) * MC, MC), MC)

    def columns_of(m):
        return pl.ds(pl.multiple_of(m * cols, cols), cols)

    def send2(c):
        return remote(
            anom.at[:, members_of(c, odd), :], r2.at[:, members_of(c, 0), :],
            s2.at[c], q2.at[c], at(-2 * sign, 0),
        )

    def send3(m):
        return remote(
            anom.at[:, members_of(last, odd), columns_of(m)],
            r2.at[:, members_of(last, 0), columns_of(m)],
            s3.at[m], q3.at[m], at(-2 * sign, 0),
        )

    def send1(c):
        return remote(
            anom.at[:, members_of(c, 1 - odd), :], r1.at[:, members_of(c, 0), :],
            s1.at[c], q1.at[c], at(sign, 0),
        )

    def to(u):
        return sign if u == 1 else -2 * sign

    def send_tab(u):
        return remote(near_far.at[u - 1], tab_in.at[u - 1], tab_s.at[u - 1], tab_r.at[u - 1], at(to(u), 0))

    def send_innov(u):
        where = columns_of(me) if u == 2 else pl.ds(0, width)
        return remote(
            innov.at[:, where], innov_in.at[u - 1, :, where], in_s.at[u - 1], in_r.at[u - 1], at(to(u), 0)
        )

    def share_innov(k, owner):
        where = columns_of(owner)
        return remote(
            innov_in.at[1, :, where], innov_in.at[1, :, where], fs.at[k], fr.at[k], at(0, k)
        )

    def send_part(u, m):
        return remote(
            part.at[u, m], got.at[u, me], ps.at[u, m], pr.at[u, me],
            ((d + (0, sign, 2 * sign)[u] + states) % states, m),
        )

    def part_from(u, m):
        return remote(part.at[u, m], got.at[u, m], ps.at[u, m], pr.at[u, m], at(sign, 0))

    def give(u, m):
        if u:
            send_part(u, m).start()
        else:
            @pl.when(m != me)
            def _():
                send_part(u, m).start()

    pl.semaphore_wait(barrier, len(greeted))
    send2(0).start()
    send1(0).start()
    for load in (load_n, load_x, load_p, load_c, load_v, load_a, load_t):
        load.start()
    acc[...] = jnp.zeros_like(acc)

    load_n.wait()
    load_x.wait()
    load_p.wait()
    row = lax.broadcasted_iota(jnp.int32, (blocks, slots), 0)
    slot = lax.broadcasted_iota(jnp.int32, (blocks, slots), 1)
    count = jnp.zeros((blocks, slots), jnp.int32)
    for i in range(blocks):
        count = jnp.where(row == i, cnt[i], count)
    valid = slot < count
    block = nbr[...]
    home = lax.div(block, jnp.int32(blocks))
    base = tix[...] * (3 * blocks) + block - home * blocks
    gap = home - d
    gap = jnp.where(gap > HOPS, gap - states, jnp.where(gap < -HOPS, gap + states, gap)) * sign
    near = jnp.where(gap == 1, base, jnp.where(gap == -1, base + 2 * blocks, none))
    far = jnp.where(gap == -2, base, jnp.where(gap == -1, base + blocks, none))
    near_far[...] = jnp.full(near_far.shape, none, jnp.int32)
    local[...] = jnp.full(local.shape, none, jnp.int32)
    near_far[0, :, 0:slots] = jnp.where(valid, near, none)
    near_far[1, :, 0:slots] = jnp.where(valid, far, none)
    local[0, :, 0:slots] = jnp.where(valid & (gap >= 0), base + gap * blocks, none)
    local[1, :, 0:slots] = jnp.where(valid & (gap == 0), base, none)
    local[2, :, 0:slots] = jnp.where(valid & (gap == 2), base + 2 * blocks, none)
    load_tab = pltpu.make_async_copy(local, tab0, obs_s.at[5])
    load_tab.start()
    for u in (1, 2):
        send_tab(u).start()

    def hot_row(k, carry):
        cell = cells[pl.ds(k, 1), :]
        value = values[pl.ds(k, 1), :]
        lo = cell & (LANES - 1)
        block = cell // width
        group = (cell // LANES) % groups
        hi = group * blocks + block
        v1 = value.astype(jnp.bfloat16).astype(jnp.float32)
        rest = value - v1
        v2 = rest.astype(jnp.bfloat16).astype(jnp.float32)
        v3 = rest - v2
        rows = blocks * groups
        same = lax.broadcasted_iota(jnp.int32, (rows, LANES), 0) == hi
        where = pl.ds(pl.multiple_of(k * LANES, LANES), LANES)
        for n, v in enumerate((v1, v2, v3)):
            hot[pl.ds(n * rows, rows), where] = jnp.where(
                same, jnp.broadcast_to(v, (rows, LANES)), 0.0
            ).astype(jnp.bfloat16)
        low[:, where] = jnp.where(
            lax.broadcasted_iota(jnp.int32, (LANES, LANES), 0) == lo, 1.0, 0.0
        ).astype(jnp.bfloat16)
        return carry

    load_c.wait()
    load_v.wait()
    lax.fori_loop(0, cells.shape[0], hot_row, 0)
    rows = blocks * groups
    sums = lax.dot_general(
        hot[...], low[...], (((1,), (1,)), ((), ())), preferred_element_type=jnp.float32
    )
    total = sums[0:rows] + sums[rows : 2 * rows] + sums[2 * rows : 3 * rows]
    for g in range(groups):
        innov[:, g * LANES : (g + 1) * LANES] = total[g * blocks : (g + 1) * blocks]
    for u in (1, 2):
        send_innov(u).start()
    for c in range(1, last):
        send2(c).start()
    for m in range(members):
        send3(m).start()
    for c in range(1, heavy):
        send1(c).start()
    for k in range(1, members):
        pl.semaphore_signal(peers, inc=1, device_id=at(0, k), device_id_type=MESH)

    load_a.wait()
    for c in range(chunks):
        for j in range(blocks):
            own_w[c, j] = (
                av[j, members_of(c, odd), :].astype(jnp.float32) * innov[pl.ds(j, 1), :]
            ).astype(jnp.bfloat16)
    load_t.wait()
    nw = width // 2

    def own_z(n, carry):
        t, x = n // 2, n % 2
        where = pl.ds(pl.multiple_of(x * nw, nw), nw)
        res = lax.dot_general(
            own_w[...].reshape(chunks * blocks * MC, width), tv[t, where, :],
            (((1,), (1,)), ((), ())), preferred_element_type=jnp.float32,
        )
        z[:, pl.ds(t * 3 * blocks, blocks), :, where] = res.reshape(chunks, blocks, MC, nw)
        return carry

    lax.fori_loop(0, KT * 2, own_z, 0)
    for c in range(heavy, chunks):
        for t in range(KT):
            z[c, (t * 3 + 1) * blocks : (t * 3 + 2) * blocks] = jnp.zeros((blocks, MC, width), jnp.float32)
    for c in range(chunks):
        z[c, none] = jnp.zeros((MC, width), jnp.float32)

    send_innov(2).wait_recv()
    for k in range(1, members):
        share_innov(k, me).start()

    load_tab.wait()
    for u in (1, 2):
        send_tab(u).wait_recv()
        fill = pltpu.make_async_copy(tab_in.at[u - 1], idx.at[u - 1], idx_s.at[u - 1])
        fill.start()
        fill.wait()

    def offset_slot(g):
        return {-2: 1 + 3 * odd, -1: 2 + odd, 1: 3 - odd, 2: 4 - 3 * odd}[g]

    free = list(range(fixed, slots))

    def spread(c, table, i, named):
        total = z[c, table(i, named[0])]
        for s in named[1:] + free:
            total = total + z[c, table(i, s)]
        return total

    def pairs(c, u, table, named, source, shift):
        def one(i, carry):
            value = source[i, members_of(c, shift), :].astype(jnp.float32) * spread(c, table, i, named)
            acc[u, i] += jnp.sum(value.reshape(MC // 8, 8, width), axis=0)
            return carry

        lax.fori_loop(0, blocks, one, 0)

    def table0(k):
        return lambda i, s: tab0[k, i, s]

    def table_in(u):
        return lambda i, s: idx[u - 1, i, s]

    def fold(u):
        for i in range(blocks):
            line = jnp.sum(acc[u, i], axis=0, keepdims=True)
            for m in range(members):
                part[u, m, i : i + 1, :] = line[:, m * cols : (m + 1) * cols]

    def far_z(c, first):
        for g, r in enumerate((r1, r2)):
            if g or not first:
                for j in range(blocks):
                    wr[g * blocks + j] = (
                        r[j, members_of(c, 0), :].astype(jnp.float32)
                        * innov_in[g, pl.ds(j, 1), :]
                    ).astype(jnp.bfloat16)
        count = 2 * blocks - first

        def one(n, carry):
            t, x = n // 2, n % 2
            where = pl.ds(pl.multiple_of(x * nw, nw), nw)
            res = lax.dot_general(
                wr[pl.ds(first, count)].reshape(count * MC, width), tv[t, where, :],
                (((1,), (1,)), ((), ())), preferred_element_type=jnp.float32,
            )
            z[c, pl.ds(t * 3 * blocks + blocks + first, count), :, where] = res.reshape(
                count, MC, nw
            )
            return carry

        lax.fori_loop(0, KT * 2, one, 0)

    def full_step(c, carry):
        send2(c).wait_recv()
        send1(c).wait_recv()
        far_z(c, 0)
        pairs(c, 2, table_in(2), [offset_slot(-2), offset_slot(-1)], r2, 0)
        pairs(c, 1, table_in(1), [offset_slot(-1), offset_slot(1)], r1, 0)
        pairs(c, 0, table0(0), [0, offset_slot(1), offset_slot(2)], av, odd)
        return carry

    send_innov(1).wait_recv()
    for k in range(1, members):
        share_innov(k, (me + members - k) % members).wait_recv()
    lax.fori_loop(0, heavy, full_step, 0)
    fold(1)
    pl.semaphore_wait(peers, members - 1)
    for m in range(members):
        give(1, m)

    def light_step(c, carry):
        send2(c).wait_recv()
        far_z(c, blocks)
        pairs(c, 2, table_in(2), [offset_slot(-2)], r2, 0)
        pairs(c, 0, table0(0), [0, offset_slot(2)], av, odd)
        return carry

    lax.fori_loop(heavy, last, light_step, 0)

    def ahead(i, carry):
        v2[i] = spread(last, table_in(2), i, [offset_slot(-2)])
        return carry

    lax.fori_loop(0, blocks, ahead, 0)
    pairs(last, 0, table0(1), [0], av, odd)
    def fold_columns(u, m, i, value):
        where = slice(m * cols, (m + 1) * cols)
        line = acc[u, i, :, where] + jnp.sum(value.reshape(MC // 8, 8, cols), axis=0)
        part[u, m, i : i + 1, :] = jnp.sum(line, axis=0, keepdims=True)

    for m in range(members):
        where = slice(m * cols, (m + 1) * cols)
        send3(m).wait_recv()
        for i in range(blocks):
            fold_columns(
                2, m, i, r2[i, members_of(last, 0), where].astype(jnp.float32) * v2[i, :, where]
            )
        give(2, m)
        for j in range(blocks):
            wr[blocks + j, :, where] = (
                r2[j, members_of(last, 0), where].astype(jnp.float32) * innov_in[1, pl.ds(j, 1), where]
            ).astype(jnp.bfloat16)

    for m in range(members):
        where = slice(m * cols, (m + 1) * cols)
        for t in range(KT):
            res = lax.dot_general(
                wr[pl.ds(blocks, blocks)].reshape(blocks * MC, width), tv[t, where, :],
                (((1,), (1,)), ((), ())), preferred_element_type=jnp.float32,
            )
            z[last, (t * 3 + 2) * blocks : (t * 3 + 3) * blocks, :, where] = res.reshape(blocks, MC, cols)
        for i in range(blocks):
            total = z[last, tab0[2, i, offset_slot(2)], :, where]
            for s in free:
                total = total + z[last, tab0[2, i, s], :, where]
            fold_columns(0, m, i, av[i, members_of(last, odd), where].astype(jnp.float32) * total)
        give(0, m)
    for u in (1, 2):
        send_tab(u).wait_send()
        send_innov(u).wait_send()
    for c in range(last):
        send2(c).wait_send()
    for m in range(members):
        send3(m).wait_send()
    for k in range(1, members):
        share_innov(k, me).wait_send()
    for c in range(heavy):
        send1(c).wait_send()
    for u in (1, 2):
        for m in range(members):
            send_part(u, m).wait_send()
    total = part[0, me]
    for u in (1, 2):
        for m in range(members):
            part_from(u, m).wait_recv()
            total = total + got[u, m]
    for k in range(1, members):
        m = (me + k) % members
        part_from(0, m).wait_recv()
        total = total + got[0, m]
    out[...] = total / jnp.float32(M - 1)
    for k in range(1, members):
        send_part(0, (me + k) % members).wait_send()


def on_device(states, members, anomalies, tapers, nbr_block, taper_index, pair_count, obs_cell, obs_value):
    blocks, mem, width = anomalies.shape
    slots = nbr_block.shape[1]
    chunks = mem // MC
    cols = width // members
    cells = obs_cell.reshape(-1, LANES)
    values = obs_value.reshape(-1, LANES)
    rows = blocks * (width // LANES)
    dma = pltpu.SemaphoreType.DMA
    any_space = pl.BlockSpec(memory_space=pl.ANY)
    vmem = pl.BlockSpec(memory_space=pltpu.VMEM)
    return pl.pallas_call(
        functools.partial(kernel, states, members, slots),
        out_shape=pltpu.VMEM((blocks, cols), jnp.float32),
        in_specs=[any_space] * 7,
        out_specs=vmem,
        scratch_shapes=[
            pltpu.VMEM(nbr_block.shape, jnp.int32),
            pltpu.VMEM(taper_index.shape, jnp.int32),
            pltpu.SMEM(pair_count.shape, jnp.int32),
            pltpu.VMEM((2, blocks, LANES), jnp.int32),
            pltpu.VMEM((3, blocks, LANES), jnp.int32),
            pltpu.SMEM((3, blocks, LANES), jnp.int32),
            pltpu.VMEM(cells.shape, jnp.int32),
            pltpu.VMEM(values.shape, jnp.float32),
            dma((6,)),
            pltpu.VMEM((blocks, mem, width), jnp.bfloat16),
            pltpu.VMEM(tapers.shape, jnp.bfloat16),
            pltpu.VMEM((blocks, mem, width), jnp.bfloat16),
            pltpu.VMEM((blocks, mem, width), jnp.bfloat16),
            pltpu.VMEM((2, blocks, LANES), jnp.int32),
            pltpu.SMEM((2, blocks, LANES), jnp.int32),
            pltpu.VMEM((blocks, width), jnp.float32),
            pltpu.VMEM((2, blocks, width), jnp.float32),
            pltpu.VMEM((3 * rows, obs_cell.shape[0]), jnp.bfloat16),
            pltpu.VMEM((LANES, obs_cell.shape[0]), jnp.bfloat16),
            pltpu.VMEM((chunks, KT * 3 * blocks + 1, MC, width), jnp.float32),
            pltpu.VMEM((chunks, blocks, MC, width), jnp.bfloat16),
            pltpu.VMEM((2 * blocks, MC, width), jnp.bfloat16),
            pltpu.VMEM((blocks, MC, width), jnp.float32),
            pltpu.VMEM((3, blocks, 8, width), jnp.float32),
            pltpu.VMEM((3, members, blocks, cols), jnp.float32),
            pltpu.VMEM((3, members, blocks, cols), jnp.float32),
            dma((2,)), dma((2,)), dma((2,)), dma, dma,
            dma((chunks,)), dma((chunks,)),
            dma((chunks,)), dma((chunks,)),
            dma((members,)), dma((members,)),
            dma((2,)), dma((2,)),
            dma((members,)), dma((members,)),
            dma((3, members)), dma((3, members)),
            pltpu.SemaphoreType.REGULAR,
        ],
        compiler_params=pltpu.CompilerParams(
            collective_id=0, has_side_effects=True, vmem_limit_bytes=66_000_000
        ),
    )(nbr_block, taper_index, pair_count, cells, values, anomalies, tapers)


def solution(mesh):
    placed = (
        P("state", "member", None),
        P(),
        P("state", None),
        P("state", None),
        P("state"),
        P("state"),
        P("state"),
    )
    return jax.shard_map(
        functools.partial(on_device, mesh.shape["state"], mesh.shape["member"]),
        mesh=mesh, in_specs=placed, out_specs=P("state", "member"), check_vma=False,
    )
```

```python
import functools

import jax
import jax.numpy as jnp
from jax import lax
from jax.experimental import pallas as pl
from jax.experimental.pallas import tpu as pltpu
from jax.sharding import PartitionSpec as P

M = 256
HOPS = 2
KT = 2
LANES = 128
MC = 16
MESH = pl.DeviceIdType.MESH


def kernel(
    states, members, slots,
    nbr_hbm, tix_hbm, cnt_hbm, cells_hbm, values_hbm, anom, tapers, out,
    nbr, tix, cnt, near_far, local, tab0, cells, values, obs_s, av, tv, r1, r2, tab_in, idx, innov, innov_in,
    hot, low, z, own_w, wr, v2, acc, part, got,
    tab_s, tab_r, idx_s, av_s, tv_s, s1, q1, s2, q2, s3, q3, in_s, in_r, fs, fr, ps, pr, peers,
):
    blocks, mem, width = anom.shape
    chunks = mem // MC
    last = chunks - 1
    groups = width // LANES
    cols = width // members
    none = KT * 3 * blocks
    d = lax.axis_index("state")
    me = lax.axis_index("member")
    odd = d % 2
    sign = 1 - 2 * odd
    heavy = chunks // 2
    fixed = 2 * HOPS + 1

    def at(ds, dm):
        return ((d + ds + states) % states, (me + dm) % members)

    barrier = pltpu.get_barrier_semaphore()
    greeted = [(sign, 0), (2, 0), (-2, 0)] + [(0, k) for k in range(1, members)]
    for ds, dm in greeted:
        pl.semaphore_signal(barrier, inc=1, device_id=at(ds, dm), device_id_type=MESH)

    load_n = pltpu.make_async_copy(nbr_hbm, nbr, obs_s.at[2])
    load_x = pltpu.make_async_copy(tix_hbm, tix, obs_s.at[3])
    load_p = pltpu.make_async_copy(cnt_hbm, cnt, obs_s.at[4])
    load_a = pltpu.make_async_copy(anom, av, av_s)
    load_t = pltpu.make_async_copy(tapers, tv, tv_s)
    load_c = pltpu.make_async_copy(cells_hbm, cells, obs_s.at[0])
    load_v = pltpu.make_async_copy(values_hbm, values, obs_s.at[1])

    def remote(src, dst, send, recv, target):
        return pltpu.make_async_remote_copy(
            src_ref=src, dst_ref=dst, send_sem=send, recv_sem=recv,
            device_id=target, device_id_type=MESH,
        )

    def members_of(c, shift):
        return pl.ds(pl.multiple_of(((c + shift * heavy) % chunks) * MC, MC), MC)

    def columns_of(m):
        return pl.ds(pl.multiple_of(m * cols, cols), cols)

    def send2(c):
        return remote(
            anom.at[:, members_of(c, odd), :], r2.at[:, members_of(c, 0), :],
            s2.at[c], q2.at[c], at(-2 * sign, 0),
        )

    def send3(m):
        return remote(
            anom.at[:, members_of(last, odd), columns_of(m)],
            r2.at[:, members_of(last, 0), columns_of(m)],
            s3.at[m], q3.at[m], at(-2 * sign, 0),
        )

    def send1(c):
        return remote(
            anom.at[:, members_of(c, 1 - odd), :], r1.at[:, members_of(c, 0), :],
            s1.at[c], q1.at[c], at(sign, 0),
        )

    def to(u):
        return sign if u == 1 else -2 * sign

    def send_tab(u):
        return remote(near_far.at[u - 1], tab_in.at[u - 1], tab_s.at[u - 1], tab_r.at[u - 1], at(to(u), 0))

    def send_innov(u):
        where = columns_of(me) if u == 2 else pl.ds(0, width)
        return remote(
            innov.at[:, where], innov_in.at[u - 1, :, where], in_s.at[u - 1], in_r.at[u - 1], at(to(u), 0)
        )

    def share_innov(k, owner):
        where = columns_of(owner)
        return remote(
            innov_in.at[1, :, where], innov_in.at[1, :, where], fs.at[k], fr.at[k], at(0, k)
        )

    def send_part(u, m):
        return remote(
            part.at[u, m], got.at[u, me], ps.at[u, m], pr.at[u, me],
            ((d + (0, sign, 2 * sign)[u] + states) % states, m),
        )

    def part_from(u, m):
        return remote(part.at[u, m], got.at[u, m], ps.at[u, m], pr.at[u, m], at(sign, 0))

    def give(u, m):
        if u:
            send_part(u, m).start()
        else:
            @pl.when(m != me)
            def _():
                send_part(u, m).start()

    pl.semaphore_wait(barrier, len(greeted))
    send2(0).start()
    send1(0).start()
    for load in (load_n, load_x, load_p, load_c, load_v, load_a, load_t):
        load.start()
    acc[...] = jnp.zeros_like(acc)

    load_n.wait()
    load_x.wait()
    load_p.wait()
    row = lax.broadcasted_iota(jnp.int32, (blocks, slots), 0)
    slot = lax.broadcasted_iota(jnp.int32, (blocks, slots), 1)
    count = jnp.zeros((blocks, slots), jnp.int32)
    for i in range(blocks):
        count = jnp.where(row == i, cnt[i], count)
    valid = slot < count
    block = nbr[...]
    home = lax.div(block, jnp.int32(blocks))
    base = tix[...] * (3 * blocks) + block - home * blocks
    gap = home - d
    gap = jnp.where(gap > HOPS, gap - states, jnp.where(gap < -HOPS, gap + states, gap)) * sign
    near = jnp.where(gap == 1, base, jnp.where(gap == -1, base + 2 * blocks, none))
    far = jnp.where(gap == -2, base, jnp.where(gap == -1, base + blocks, none))
    near_far[...] = jnp.full(near_far.shape, none, jnp.int32)
    local[...] = jnp.full(local.shape, none, jnp.int32)
    near_far[0, :, 0:slots] = jnp.where(valid, near, none)
    near_far[1, :, 0:slots] = jnp.where(valid, far, none)
    local[0, :, 0:slots] = jnp.where(valid & (gap >= 0), base + gap * blocks, none)
    local[1, :, 0:slots] = jnp.where(valid & (gap == 0), base, none)
    local[2, :, 0:slots] = jnp.where(valid & (gap == 2), base + 2 * blocks, none)
    load_tab = pltpu.make_async_copy(local, tab0, obs_s.at[5])
    load_tab.start()
    for u in (1, 2):
        send_tab(u).start()

    def hot_row(k, carry):
        cell = cells[pl.ds(k, 1), :]
        value = values[pl.ds(k, 1), :]
        lo = cell & (LANES - 1)
        block = cell // width
        group = (cell // LANES) % groups
        hi = group * blocks + block
        v1 = value.astype(jnp.bfloat16).astype(jnp.float32)
        rest = value - v1
        v2 = rest.astype(jnp.bfloat16).astype(jnp.float32)
        v3 = rest - v2
        rows = blocks * groups
        same = lax.broadcasted_iota(jnp.int32, (rows, LANES), 0) == hi
        where = pl.ds(pl.multiple_of(k * LANES, LANES), LANES)
        for n, v in enumerate((v1, v2, v3)):
            hot[pl.ds(n * rows, rows), where] = jnp.where(
                same, jnp.broadcast_to(v, (rows, LANES)), 0.0
            ).astype(jnp.bfloat16)
        low[:, where] = jnp.where(
            lax.broadcasted_iota(jnp.int32, (LANES, LANES), 0) == lo, 1.0, 0.0
        ).astype(jnp.bfloat16)
        return carry

    load_c.wait()
    load_v.wait()
    lax.fori_loop(0, cells.shape[0], hot_row, 0)
    rows = blocks * groups
    sums = lax.dot_general(
        hot[...], low[...], (((1,), (1,)), ((), ())), preferred_element_type=jnp.float32
    )
    total = sums[0:rows] + sums[rows : 2 * rows] + sums[2 * rows : 3 * rows]
    for g in range(groups):
        innov[:, g * LANES : (g + 1) * LANES] = total[g * blocks : (g + 1) * blocks]
    for u in (1, 2):
        send_innov(u).start()
    for c in range(1, last):
        send2(c).start()
    for m in range(members):
        send3(m).start()
    for c in range(1, heavy):
        send1(c).start()
    for k in range(1, members):
        pl.semaphore_signal(peers, inc=1, device_id=at(0, k), device_id_type=MESH)

    load_a.wait()
    for c in range(chunks):
        for j in range(blocks):
            own_w[c, j] = (
                av[j, members_of(c, odd), :].astype(jnp.float32) * innov[pl.ds(j, 1), :]
            ).astype(jnp.bfloat16)
    load_t.wait()
    nw = width // 2

    def own_z(n, carry):
        t, x = n // 2, n % 2
        where = pl.ds(pl.multiple_of(x * nw, nw), nw)
        res = lax.dot_general(
            own_w[...].reshape(chunks * blocks * MC, width), tv[t, where, :],
            (((1,), (1,)), ((), ())), preferred_element_type=jnp.float32,
        )
        z[:, pl.ds(t * 3 * blocks, blocks), :, where] = res.reshape(chunks, blocks, MC, nw)
        return carry

    lax.fori_loop(0, KT * 2, own_z, 0)
    for c in range(heavy, chunks):
        for t in range(KT):
            z[c, (t * 3 + 1) * blocks : (t * 3 + 2) * blocks] = jnp.zeros((blocks, MC, width), jnp.float32)
    for c in range(chunks):
        z[c, none] = jnp.zeros((MC, width), jnp.float32)

    send_innov(2).wait_recv()
    for k in range(1, members):
        share_innov(k, me).start()

    load_tab.wait()
    for u in (1, 2):
        send_tab(u).wait_recv()
        fill = pltpu.make_async_copy(tab_in.at[u - 1], idx.at[u - 1], idx_s.at[u - 1])
        fill.start()
        fill.wait()

    def offset_slot(g):
        return {-2: 1 + 3 * odd, -1: 2 + odd, 1: 3 - odd, 2: 4 - 3 * odd}[g]

    free = list(range(fixed, slots))

    def spread(c, table, i, named):
        total = z[c, table(i, named[0])]
        for s in named[1:] + free:
            total = total + z[c, table(i, s)]
        return total

    def pairs(c, u, table, named, source, shift):
        def one(i, carry):
            value = source[i, members_of(c, shift), :].astype(jnp.float32) * spread(c, table, i, named)
            acc[u, i] += jnp.sum(value.reshape(MC // 8, 8, width), axis=0)
            return carry

        lax.fori_loop(0, blocks, one, 0)

    def table0(k):
        return lambda i, s: tab0[k, i, s]

    def table_in(u):
        return lambda i, s: idx[u - 1, i, s]

    def fold(u):
        for i in range(blocks):
            line = jnp.sum(acc[u, i], axis=0, keepdims=True)
            for m in range(members):
                part[u, m, i : i + 1, :] = line[:, m * cols : (m + 1) * cols]

    def far_z(c, first):
        for g, r in enumerate((r1, r2)):
            if g or not first:
                for j in range(blocks):
                    wr[g * blocks + j] = (
                        r[j, members_of(c, 0), :].astype(jnp.float32)
                        * innov_in[g, pl.ds(j, 1), :]
                    ).astype(jnp.bfloat16)
        count = 2 * blocks - first

        def one(n, carry):
            t, x = n // 2, n % 2
            where = pl.ds(pl.multiple_of(x * nw, nw), nw)
            res = lax.dot_general(
                wr[pl.ds(first, count)].reshape(count * MC, width), tv[t, where, :],
                (((1,), (1,)), ((), ())), preferred_element_type=jnp.float32,
            )
            z[c, pl.ds(t * 3 * blocks + blocks + first, count), :, where] = res.reshape(
                count, MC, nw
            )
            return carry

        lax.fori_loop(0, KT * 2, one, 0)

    def full_step(c, carry):
        send2(c).wait_recv()
        send1(c).wait_recv()
        far_z(c, 0)
        pairs(c, 2, table_in(2), [offset_slot(-2), offset_slot(-1)], r2, 0)
        pairs(c, 1, table_in(1), [offset_slot(-1), offset_slot(1)], r1, 0)
        pairs(c, 0, table0(0), [0, offset_slot(1), offset_slot(2)], av, odd)
        return carry

    def ahead(c, carry):
        def one(i, carry):
            v2[c - heavy, i] = spread(c, table_in(2), i, [offset_slot(-2)])
            return carry

        lax.fori_loop(0, blocks, one, 0)
        pairs(c, 0, table0(1), [0], av, odd)
        return carry

    lax.fori_loop(heavy, chunks, ahead, 0)
    send_innov(1).wait_recv()
    for k in range(1, members):
        share_innov(k, (me + members - k) % members).wait_recv()
    lax.fori_loop(0, heavy, full_step, 0)
    fold(1)
    pl.semaphore_wait(peers, members - 1)
    for m in range(members):
        give(1, m)

    def reach(c):
        def one(i, carry):
            value = r2[i, members_of(c, 0), :].astype(jnp.float32) * v2[c - heavy, i]
            acc[2, i] += jnp.sum(value.reshape(MC // 8, 8, width), axis=0)
            return carry

        lax.fori_loop(0, blocks, one, 0)

    def light_step(c, carry):
        send2(c).wait_recv()
        reach(c)
        far_z(c, blocks)
        return carry

    lax.fori_loop(heavy, last, light_step, 0)

    def fold_columns(u, m, i, value):
        where = slice(m * cols, (m + 1) * cols)
        line = acc[u, i, :, where] + jnp.sum(value.reshape(MC // 8, 8, cols), axis=0)
        part[u, m, i : i + 1, :] = jnp.sum(line, axis=0, keepdims=True)

    def depth_z(m, t, where):
        inner = slice(m * cols, (m + 1) * cols)
        res = lax.dot_general(
            wr[blocks : 2 * blocks, :, inner].reshape(blocks * MC, cols), tv[t, where, inner],
            (((1,), (1,)), ((), ())), preferred_element_type=jnp.float32,
        ).reshape(blocks, MC, where.stop - where.start)
        panels = slice((t * 3 + 2) * blocks, (t * 3 + 3) * blocks)
        if m:
            res = z[last, panels, :, where] + res
        z[last, panels, :, where] = res

    for m in range(members):
        where = slice(m * cols, (m + 1) * cols)
        send3(m).wait_recv()
        for i in range(blocks):
            fold_columns(
                2, m, i, r2[i, members_of(last, 0), where].astype(jnp.float32) * v2[last - heavy, i, :, where]
            )
        give(2, m)
        for j in range(blocks):
            wr[blocks + j, :, where] = (
                r2[j, members_of(last, 0), where].astype(jnp.float32) * innov_in[1, pl.ds(j, 1), where]
            ).astype(jnp.bfloat16)
        if m < members - 1:
            for t in range(KT):
                for x in range(members):
                    depth_z(m, t, slice(x * cols, (x + 1) * cols))
        if m == members - 2:
            for c in range(heavy, last):
                pairs(c, 0, table0(2), [offset_slot(2)], av, odd)

    for m in range(members):
        where = slice(m * cols, (m + 1) * cols)
        for t in range(KT):
            depth_z(members - 1, t, where)
        for i in range(blocks):
            total = z[last, tab0[2, i, offset_slot(2)], :, where]
            for s in free:
                total = total + z[last, tab0[2, i, s], :, where]
            fold_columns(0, m, i, av[i, members_of(last, odd), where].astype(jnp.float32) * total)
        give(0, m)
    for u in (1, 2):
        send_tab(u).wait_send()
        send_innov(u).wait_send()
    for c in range(last):
        send2(c).wait_send()
    for m in range(members):
        send3(m).wait_send()
    for k in range(1, members):
        share_innov(k, me).wait_send()
    for c in range(heavy):
        send1(c).wait_send()
    for u in (1, 2):
        for m in range(members):
            send_part(u, m).wait_send()
    total = part[0, me]
    for u in (1, 2):
        for m in range(members):
            part_from(u, m).wait_recv()
            total = total + got[u, m]
    for k in range(1, members):
        m = (me + k) % members
        part_from(0, m).wait_recv()
        total = total + got[0, m]
    out[...] = total / jnp.float32(M - 1)
    for k in range(1, members):
        send_part(0, (me + k) % members).wait_send()


def on_device(states, members, anomalies, tapers, nbr_block, taper_index, pair_count, obs_cell, obs_value):
    blocks, mem, width = anomalies.shape
    slots = nbr_block.shape[1]
    chunks = mem // MC
    cols = width // members
    cells = obs_cell.reshape(-1, LANES)
    values = obs_value.reshape(-1, LANES)
    rows = blocks * (width // LANES)
    dma = pltpu.SemaphoreType.DMA
    any_space = pl.BlockSpec(memory_space=pl.ANY)
    vmem = pl.BlockSpec(memory_space=pltpu.VMEM)
    return pl.pallas_call(
        functools.partial(kernel, states, members, slots),
        out_shape=pltpu.VMEM((blocks, cols), jnp.float32),
        in_specs=[any_space] * 7,
        out_specs=vmem,
        scratch_shapes=[
            pltpu.VMEM(nbr_block.shape, jnp.int32),
            pltpu.VMEM(taper_index.shape, jnp.int32),
            pltpu.SMEM(pair_count.shape, jnp.int32),
            pltpu.VMEM((2, blocks, LANES), jnp.int32),
            pltpu.VMEM((3, blocks, LANES), jnp.int32),
            pltpu.SMEM((3, blocks, LANES), jnp.int32),
            pltpu.VMEM(cells.shape, jnp.int32),
            pltpu.VMEM(values.shape, jnp.float32),
            dma((6,)),
            pltpu.VMEM((blocks, mem, width), jnp.bfloat16),
            pltpu.VMEM(tapers.shape, jnp.bfloat16),
            pltpu.VMEM((blocks, mem, width), jnp.bfloat16),
            pltpu.VMEM((blocks, mem, width), jnp.bfloat16),
            pltpu.VMEM((2, blocks, LANES), jnp.int32),
            pltpu.SMEM((2, blocks, LANES), jnp.int32),
            pltpu.VMEM((blocks, width), jnp.float32),
            pltpu.VMEM((2, blocks, width), jnp.float32),
            pltpu.VMEM((3 * rows, obs_cell.shape[0]), jnp.bfloat16),
            pltpu.VMEM((LANES, obs_cell.shape[0]), jnp.bfloat16),
            pltpu.VMEM((chunks, KT * 3 * blocks + 1, MC, width), jnp.float32),
            pltpu.VMEM((chunks, blocks, MC, width), jnp.bfloat16),
            pltpu.VMEM((2 * blocks, MC, width), jnp.bfloat16),
            pltpu.VMEM((chunks // 2, blocks, MC, width), jnp.float32),
            pltpu.VMEM((3, blocks, 8, width), jnp.float32),
            pltpu.VMEM((3, members, blocks, cols), jnp.float32),
            pltpu.VMEM((3, members, blocks, cols), jnp.float32),
            dma((2,)), dma((2,)), dma((2,)), dma, dma,
            dma((chunks,)), dma((chunks,)),
            dma((chunks,)), dma((chunks,)),
            dma((members,)), dma((members,)),
            dma((2,)), dma((2,)),
            dma((members,)), dma((members,)),
            dma((3, members)), dma((3, members)),
            pltpu.SemaphoreType.REGULAR,
        ],
        compiler_params=pltpu.CompilerParams(
            collective_id=0, has_side_effects=True, vmem_limit_bytes=66_000_000
        ),
    )(nbr_block, taper_index, pair_count, cells, values, anomalies, tapers)


def solution(mesh):
    placed = (
        P("state", "member", None),
        P(),
        P("state", None),
        P("state", None),
        P("state"),
        P("state"),
        P("state"),
    )
    return jax.shard_map(
        functools.partial(on_device, mesh.shape["state"], mesh.shape["member"]),
        mesh=mesh, in_specs=placed, out_specs=P("state", "member"), check_vma=False,
    )
```

```python
import functools

import jax
import jax.numpy as jnp
from jax import lax
from jax.experimental import pallas as pl
from jax.experimental.pallas import tpu as pltpu
from jax.sharding import PartitionSpec as P

M = 256
HOPS = 2
KT = 2
LANES = 128
MC = 16
CORES = 2
MESH = pl.DeviceIdType.MESH


def kernel(
    states, members, slots,
    nbr_hbm, tix_hbm, cnt_hbm, cells_hbm, values_hbm, anom, tapers, out,
    nbr, tix, cnt, near_far, local, tab0, cells, values, obs_s, av, tv, r1, r2, tab_in, idx, innov, innov_in,
    hot, low, z, own_w, wr, v2, acc, part, got,
    tab_s, tab_r, idx_s, av_s, tv_s, s1, q1, s2, q2, s3, q3, relay_s, in_s, in_r, fs, fr, ps, pr, peers,
):
    blocks, mem, width = anom.shape
    chunks = mem // MC
    last = chunks - 1
    groups = width // LANES
    cols = width // members
    none = KT * 3 * blocks
    d = lax.axis_index("state")
    me = lax.axis_index("member")
    odd = d % 2
    sign = 1 - 2 * odd
    heavy = chunks // 2
    fixed = 2 * HOPS + 1

    def at(ds, dm):
        return ((d + ds + states) % states, (me + dm) % members)

    barrier = pltpu.get_barrier_semaphore()
    greeted = [(sign, 0), (2 * sign, 0)] + [(0, k) for k in range(1, members)]
    for ds, dm in greeted:
        pl.semaphore_signal(barrier, inc=1, device_id=at(ds, dm), device_id_type=MESH)

    load_n = pltpu.make_async_copy(nbr_hbm, nbr, obs_s.at[2])
    load_x = pltpu.make_async_copy(tix_hbm, tix, obs_s.at[3])
    load_p = pltpu.make_async_copy(cnt_hbm, cnt, obs_s.at[4])
    load_a = pltpu.make_async_copy(anom, av, av_s)
    load_t = pltpu.make_async_copy(tapers, tv, tv_s)
    load_c = pltpu.make_async_copy(cells_hbm, cells, obs_s.at[0])
    load_v = pltpu.make_async_copy(values_hbm, values, obs_s.at[1])

    def remote(src, dst, send, recv, target):
        return pltpu.make_async_remote_copy(
            src_ref=src, dst_ref=dst, send_sem=send, recv_sem=recv,
            device_id=target, device_id_type=MESH,
        )

    def members_of(c, shift):
        return pl.ds(pl.multiple_of(((c + shift * heavy) % chunks) * MC, MC), MC)

    def columns_of(m):
        return pl.ds(pl.multiple_of(m * cols, cols), cols)

    def send2(c):
        return remote(
            anom.at[:, members_of(c, odd), :], r2.at[:, members_of(c, 0), :],
            s2.at[c], q2.at[c], at(-2 * sign, 0),
        )

    def send3(m):
        return remote(
            anom.at[:, members_of(last, odd), columns_of(m)],
            r2.at[:, members_of(last, 0), columns_of(m)],
            s3.at[m], q3.at[m], at(-2 * sign, 0),
        )

    def send1(c):
        return remote(
            anom.at[:, members_of(c, 1 - odd), :], r1.at[:, members_of(c, 0), :],
            s1.at[c], q1.at[c], at(sign, 0),
        )

    def relay():
        return remote(
            r1.at[:, members_of(heavy - 1, 0), columns_of(0)],
            r2.at[:, members_of(last, 0), columns_of(0)],
            relay_s, q3.at[0], at(-3, 0),
        )

    def to(u):
        return sign if u == 1 else -2 * sign

    def send_tab(u):
        return remote(near_far.at[u - 1], tab_in.at[u - 1], tab_s.at[u - 1], tab_r.at[u - 1], at(to(u), 0))

    def send_innov(u):
        where = columns_of(me) if u == 2 else pl.ds(0, width)
        return remote(
            innov.at[:, where], innov_in.at[u - 1, :, where], in_s.at[u - 1], in_r.at[u - 1], at(to(u), 0)
        )

    def share_innov(k, owner):
        where = columns_of(owner)
        return remote(
            innov_in.at[1, :, where], innov_in.at[1, :, where], fs.at[k], fr.at[k], at(0, k)
        )

    def send_part(u, m):
        return remote(
            part.at[u, m], got.at[u, me], ps.at[u, m], pr.at[u, me],
            ((d + (0, sign, 2 * sign)[u] + states) % states, m),
        )

    def part_from(u, m):
        return remote(part.at[u, m], got.at[u, m], ps.at[u, m], pr.at[u, m], at(sign, 0))

    pl.semaphore_wait(barrier, len(greeted))
    send2(0).start()
    send1(0).start()
    for load in (load_n, load_x, load_p, load_c, load_v, load_a, load_t):
        load.start()
    acc[...] = jnp.zeros_like(acc)

    load_n.wait()
    load_x.wait()
    load_p.wait()
    row = lax.broadcasted_iota(jnp.int32, (blocks, slots), 0)
    slot = lax.broadcasted_iota(jnp.int32, (blocks, slots), 1)
    count = jnp.zeros((blocks, slots), jnp.int32)
    for i in range(blocks):
        count = jnp.where(row == i, cnt[i], count)
    valid = slot < count
    block = nbr[...]
    home = lax.div(block, jnp.int32(blocks))
    base = tix[...] * (3 * blocks) + block - home * blocks
    gap = home - d
    gap = jnp.where(gap > HOPS, gap - states, jnp.where(gap < -HOPS, gap + states, gap)) * sign
    near = jnp.where(gap == 1, base, jnp.where(gap == -1, base + 2 * blocks, none))
    far = jnp.where(gap == -2, base, jnp.where(gap == -1, base + blocks, none))
    near_far[...] = jnp.full(near_far.shape, none, jnp.int32)
    local[...] = jnp.full(local.shape, none, jnp.int32)
    near_far[0, :, 0:slots] = jnp.where(valid, near, none)
    near_far[1, :, 0:slots] = jnp.where(valid, far, none)
    local[0, :, 0:slots] = jnp.where(valid & (gap >= 0), base + gap * blocks, none)
    local[1, :, 0:slots] = jnp.where(valid & (gap == 0), base, none)
    local[2, :, 0:slots] = jnp.where(valid & (gap == 2), base + 2 * blocks, none)
    load_tab = pltpu.make_async_copy(local, tab0, obs_s.at[5])
    load_tab.start()
    for u in (1, 2):
        send_tab(u).start()

    def hot_row(k, carry):
        cell = cells[pl.ds(k, 1), :]
        value = values[pl.ds(k, 1), :]
        lo = cell & (LANES - 1)
        block = cell // width
        group = (cell // LANES) % groups
        hi = group * blocks + block
        v1 = value.astype(jnp.bfloat16).astype(jnp.float32)
        rest = value - v1
        v2 = rest.astype(jnp.bfloat16).astype(jnp.float32)
        v3 = rest - v2
        rows = blocks * groups
        same = lax.broadcasted_iota(jnp.int32, (rows, LANES), 0) == hi
        where = pl.ds(pl.multiple_of(k * LANES, LANES), LANES)
        for n, v in enumerate((v1, v2, v3)):
            hot[pl.ds(n * rows, rows), where] = jnp.where(
                same, jnp.broadcast_to(v, (rows, LANES)), 0.0
            ).astype(jnp.bfloat16)
        low[:, where] = jnp.where(
            lax.broadcasted_iota(jnp.int32, (LANES, LANES), 0) == lo, 1.0, 0.0
        ).astype(jnp.bfloat16)
        return carry

    load_c.wait()
    load_v.wait()
    lax.fori_loop(0, cells.shape[0], hot_row, 0)
    rows = blocks * groups
    sums = lax.dot_general(
        hot[...], low[...], (((1,), (1,)), ((), ())), preferred_element_type=jnp.float32
    )
    total = sums[0:rows] + sums[rows : 2 * rows] + sums[2 * rows : 3 * rows]
    for g in range(groups):
        innov[:, g * LANES : (g + 1) * LANES] = total[g * blocks : (g + 1) * blocks]
    for u in (1, 2):
        send_innov(u).start()
    for c in range(1, last):
        send2(c).start()

    @pl.when(d > 1)
    def _():
        send3(0).start()

    @pl.when(d != 1)
    def _():
        for m in range(1, members):
            send3(m).start()

    for c in range(1, heavy):
        send1(c).start()

    load_a.wait()
    for c in range(chunks):
        for j in range(blocks):
            own_w[c, j] = (
                av[j, members_of(c, odd), :].astype(jnp.float32) * innov[pl.ds(j, 1), :]
            ).astype(jnp.bfloat16)
    load_t.wait()
    nw = width // 2

    def own_z(n, carry):
        t, x = n // 2, n % 2
        where = pl.ds(pl.multiple_of(x * nw, nw), nw)
        res = lax.dot_general(
            own_w[...].reshape(chunks * blocks * MC, width), tv[t, where, :],
            (((1,), (1,)), ((), ())), preferred_element_type=jnp.float32,
        )
        z[:, pl.ds(t * 3 * blocks, blocks), :, where] = res.reshape(chunks, blocks, MC, nw)
        return carry

    lax.fori_loop(0, KT * 2, own_z, 0)
    for c in range(heavy, chunks):
        for t in range(KT):
            z[c, (t * 3 + 1) * blocks : (t * 3 + 2) * blocks] = jnp.zeros((blocks, MC, width), jnp.float32)
    for c in range(chunks):
        z[c, none] = jnp.zeros((MC, width), jnp.float32)

    send_innov(2).wait_recv()
    for k in range(1, members):
        share_innov(k, me).start()

    load_tab.wait()
    for u in (1, 2):
        send_tab(u).wait_recv()
        fill = pltpu.make_async_copy(tab_in.at[u - 1], idx.at[u - 1], idx_s.at[u - 1])
        fill.start()
        fill.wait()

    def offset_slot(g):
        return {-2: 1 + 3 * odd, -1: 2 + odd, 1: 3 - odd, 2: 4 - 3 * odd}[g]

    free = list(range(fixed, slots))

    def spread(c, table, i, named):
        total = z[c, table(i, named[0])]
        for s in named[1:] + free:
            total = total + z[c, table(i, s)]
        return total

    def pairs(c, u, table, named, source, shift):
        def one(i, carry):
            value = source[i, members_of(c, shift), :].astype(jnp.float32) * spread(c, table, i, named)
            acc[u, i] += jnp.sum(value.reshape(MC // 8, 8, width), axis=0)
            return carry

        lax.fori_loop(0, blocks, one, 0)

    def table0(k):
        return lambda i, s: tab0[k, i, s]

    def table_in(u):
        return lambda i, s: idx[u - 1, i, s]

    def fold(u):
        for i in range(blocks):
            line = jnp.sum(acc[u, i], axis=0, keepdims=True)
            for m in range(members):
                part[u, m, i : i + 1, :] = line[:, m * cols : (m + 1) * cols]

    def far_z(c, first):
        for g, r in enumerate((r1, r2)):
            if g or not first:
                for j in range(blocks):
                    wr[g * blocks + j] = (
                        r[j, members_of(c, 0), :].astype(jnp.float32)
                        * innov_in[g, pl.ds(j, 1), :]
                    ).astype(jnp.bfloat16)
        count = 2 * blocks - first

        def one(n, carry):
            t, x = n // 2, n % 2
            where = pl.ds(pl.multiple_of(x * nw, nw), nw)
            res = lax.dot_general(
                wr[pl.ds(first, count)].reshape(count * MC, width), tv[t, where, :],
                (((1,), (1,)), ((), ())), preferred_element_type=jnp.float32,
            )
            z[c, pl.ds(t * 3 * blocks + blocks + first, count), :, where] = res.reshape(
                count, MC, nw
            )
            return carry

        lax.fori_loop(0, KT * 2, one, 0)

    def full_step(c, carry):
        send2(c).wait_recv()
        send1(c).wait_recv()

        @pl.when((c == heavy - 1) & (d == 1))
        def _():
            relay().start()
            for m in range(members):
                send3(m).start()

        @pl.when(c == 0)
        def _():
            for k in range(1, members):
                pl.semaphore_signal(peers, inc=1, device_id=at(0, k), device_id_type=MESH)

        far_z(c, 0)
        pairs(c, 2, table_in(2), [offset_slot(-2), offset_slot(-1)], r2, 0)
        pairs(c, 1, table_in(1), [offset_slot(-1), offset_slot(1)], r1, 0)
        pairs(c, 0, table0(0), [0, offset_slot(1), offset_slot(2)], av, odd)
        return carry

    def ahead(c, carry):
        def one(i, carry):
            v2[c - heavy, i] = spread(c, table_in(2), i, [offset_slot(-2)])
            return carry

        lax.fori_loop(0, blocks, one, 0)
        pairs(c, 0, table0(1), [0], av, odd)
        return carry

    lax.fori_loop(heavy, chunks, ahead, 0)
    send_innov(1).wait_recv()
    for k in range(1, members):
        share_innov(k, (me + members - k) % members).wait_recv()
    lax.fori_loop(0, heavy, full_step, 0)
    fold(1)
    pl.semaphore_wait(peers, members - 1)
    for m in range(members):
        send_part(1, m).start()

    def reach(c):
        def one(i, carry):
            value = r2[i, members_of(c, 0), :].astype(jnp.float32) * v2[c - heavy, i]
            acc[2, i] += jnp.sum(value.reshape(MC // 8, 8, width), axis=0)
            return carry

        lax.fori_loop(0, blocks, one, 0)

    def light_step(c, carry):
        send2(c).wait_recv()
        reach(c)
        far_z(c, blocks)
        return carry

    lax.fori_loop(heavy, last, light_step, 0)

    def fold_columns(u, m, i, value):
        where = columns_of(m)
        line = acc[u, i, :, where] + jnp.sum(value.reshape(MC // 8, 8, cols), axis=0)
        part[u, m, i : i + 1, :] = jnp.sum(line, axis=0, keepdims=True)

    def depth_z(m, t, where):
        inner = slice(m * cols, (m + 1) * cols)
        res = lax.dot_general(
            wr[blocks : 2 * blocks, :, inner].reshape(blocks * MC, cols), tv[t, where, inner],
            (((1,), (1,)), ((), ())), preferred_element_type=jnp.float32,
        ).reshape(blocks, MC, cols)
        panels = slice((t * 3 + 2) * blocks, (t * 3 + 3) * blocks)
        if m:
            res = z[last, panels, :, where] + res
        z[last, panels, :, where] = res

    for m in range(members):
        where = slice(m * cols, (m + 1) * cols)
        send3(m).wait_recv()
        for i in range(blocks):
            fold_columns(
                2, m, i, r2[i, members_of(last, 0), where].astype(jnp.float32) * v2[last - heavy, i, :, where]
            )
        send_part(2, m).start()
        for j in range(blocks):
            wr[blocks + j, :, where] = (
                r2[j, members_of(last, 0), where].astype(jnp.float32) * innov_in[1, pl.ds(j, 1), where]
            ).astype(jnp.bfloat16)
        if m < members - 1:
            for t in range(KT):
                for x in range(members):
                    depth_z(m, t, slice(x * cols, (x + 1) * cols))
        if m == members - 2:
            for c in range(heavy, last):
                pairs(c, 0, table0(2), [offset_slot(2)], av, odd)

    chips = members // CORES
    for away in range(members - 1, -1, -1):
        m = (me // CORES + away // CORES) % chips * CORES + (me + away) % CORES
        where = columns_of(m)
        for t in range(KT):
            depth_z(members - 1, t, where)
        for i in range(blocks):
            total = z[last, tab0[2, i, offset_slot(2)], :, where]
            for s in free:
                total = total + z[last, tab0[2, i, s], :, where]
            fold_columns(0, m, i, av[i, members_of(last, odd), where].astype(jnp.float32) * total)
        if away:
            send_part(0, m).start()
    for u in (1, 2):
        send_tab(u).wait_send()
        send_innov(u).wait_send()
    for c in range(last):
        send2(c).wait_send()
    for m in range(1, members):
        send3(m).wait_send()

    @pl.when(d > 0)
    def _():
        send3(0).wait_send()

    @pl.when(d == 1)
    def _():
        relay().wait_send()

    for k in range(1, members):
        share_innov(k, me).wait_send()
    for c in range(heavy):
        send1(c).wait_send()
    for u in (1, 2):
        for m in range(members):
            send_part(u, m).wait_send()
    total = part[0, me]
    for u in (1, 2):
        for m in range(members):
            part_from(u, m).wait_recv()
            total = total + got[u, m]
    for k in range(1, members):
        m = (me + k) % members
        part_from(0, m).wait_recv()
        total = total + got[0, m]
    out[...] = total / jnp.float32(M - 1)
    for k in range(1, members):
        send_part(0, (me + k) % members).wait_send()


def on_device(states, members, anomalies, tapers, nbr_block, taper_index, pair_count, obs_cell, obs_value):
    blocks, mem, width = anomalies.shape
    slots = nbr_block.shape[1]
    chunks = mem // MC
    cols = width // members
    cells = obs_cell.reshape(-1, LANES)
    values = obs_value.reshape(-1, LANES)
    rows = blocks * (width // LANES)
    dma = pltpu.SemaphoreType.DMA
    any_space = pl.BlockSpec(memory_space=pl.ANY)
    vmem = pl.BlockSpec(memory_space=pltpu.VMEM)
    return pl.pallas_call(
        functools.partial(kernel, states, members, slots),
        out_shape=pltpu.VMEM((blocks, cols), jnp.float32),
        in_specs=[any_space] * 7,
        out_specs=vmem,
        scratch_shapes=[
            pltpu.VMEM(nbr_block.shape, jnp.int32),
            pltpu.VMEM(taper_index.shape, jnp.int32),
            pltpu.SMEM(pair_count.shape, jnp.int32),
            pltpu.VMEM((2, blocks, LANES), jnp.int32),
            pltpu.VMEM((3, blocks, LANES), jnp.int32),
            pltpu.SMEM((3, blocks, LANES), jnp.int32),
            pltpu.VMEM(cells.shape, jnp.int32),
            pltpu.VMEM(values.shape, jnp.float32),
            dma((6,)),
            pltpu.VMEM((blocks, mem, width), jnp.bfloat16),
            pltpu.VMEM(tapers.shape, jnp.bfloat16),
            pltpu.VMEM((blocks, mem, width), jnp.bfloat16),
            pltpu.VMEM((blocks, mem, width), jnp.bfloat16),
            pltpu.VMEM((2, blocks, LANES), jnp.int32),
            pltpu.SMEM((2, blocks, LANES), jnp.int32),
            pltpu.VMEM((blocks, width), jnp.float32),
            pltpu.VMEM((2, blocks, width), jnp.float32),
            pltpu.VMEM((3 * rows, obs_cell.shape[0]), jnp.bfloat16),
            pltpu.VMEM((LANES, obs_cell.shape[0]), jnp.bfloat16),
            pltpu.VMEM((chunks, KT * 3 * blocks + 1, MC, width), jnp.float32),
            pltpu.VMEM((chunks, blocks, MC, width), jnp.bfloat16),
            pltpu.VMEM((2 * blocks, MC, width), jnp.bfloat16),
            pltpu.VMEM((chunks // 2, blocks, MC, width), jnp.float32),
            pltpu.VMEM((3, blocks, 8, width), jnp.float32),
            pltpu.VMEM((3, members, blocks, cols), jnp.float32),
            pltpu.VMEM((3, members, blocks, cols), jnp.float32),
            dma((2,)), dma((2,)), dma((2,)), dma, dma,
            dma((chunks,)), dma((chunks,)),
            dma((chunks,)), dma((chunks,)),
            dma((members,)), dma((members,)), dma,
            dma((2,)), dma((2,)),
            dma((members,)), dma((members,)),
            dma((3, members)), dma((3, members)),
            pltpu.SemaphoreType.REGULAR,
        ],
        compiler_params=pltpu.CompilerParams(
            collective_id=0, has_side_effects=True, vmem_limit_bytes=66_000_000
        ),
    )(nbr_block, taper_index, pair_count, cells, values, anomalies, tapers)


def solution(mesh):
    placed = (
        P("state", "member", None),
        P(),
        P("state", None),
        P("state", None),
        P("state"),
        P("state"),
        P("state"),
    )
    return jax.shard_map(
        functools.partial(on_device, mesh.shape["state"], mesh.shape["member"]),
        mesh=mesh, in_specs=placed, out_specs=P("state", "member"), check_vma=False,
    )
```

```python
import functools

import jax
import jax.numpy as jnp
from jax import lax
from jax.experimental import pallas as pl
from jax.experimental.pallas import tpu as pltpu
from jax.sharding import PartitionSpec as P

M = 256
HOPS = 2
KT = 2
LANES = 128
MC = 16
CORES = 2
MESH = pl.DeviceIdType.MESH


def kernel(
    states, members, slots,
    nbr_hbm, tix_hbm, cnt_hbm, cells_hbm, values_hbm, anom, tapers, out,
    nbr, tix, cnt, near_far, local, tab0, cells, values, obs_s, av, tv, r1, r2, tab_in, idx, innov, innov_in,
    hot, low, z, own_w, wr, v2, acc, part, got,
    tab_s, tab_r, idx_s, av_s, tv_s, s1, q1, s2, q2, s3, q3, relay_s, in_s, in_r, fs, fr, ps, pr, peers,
):
    blocks, mem, width = anom.shape
    chunks = mem // MC
    last = chunks - 1
    groups = width // LANES
    cols = width // members
    none = KT * 3 * blocks
    d = lax.axis_index("state")
    me = lax.axis_index("member")
    odd = d % 2
    sign = 1 - 2 * odd
    heavy = chunks // 2
    fixed = 2 * HOPS + 1

    def at(ds, dm):
        return ((d + ds + states) % states, (me + dm) % members)

    barrier = pltpu.get_barrier_semaphore()
    greeted = [(sign, 0), (2 * sign, 0)] + [(0, k) for k in range(1, members)]
    for ds, dm in greeted:
        pl.semaphore_signal(barrier, inc=1, device_id=at(ds, dm), device_id_type=MESH)

    load_n = pltpu.make_async_copy(nbr_hbm, nbr, obs_s.at[2])
    load_x = pltpu.make_async_copy(tix_hbm, tix, obs_s.at[3])
    load_p = pltpu.make_async_copy(cnt_hbm, cnt, obs_s.at[4])
    load_a = pltpu.make_async_copy(anom, av, av_s)
    load_t = pltpu.make_async_copy(tapers, tv, tv_s)
    load_c = pltpu.make_async_copy(cells_hbm, cells, obs_s.at[0])
    load_v = pltpu.make_async_copy(values_hbm, values, obs_s.at[1])

    def remote(src, dst, send, recv, target):
        return pltpu.make_async_remote_copy(
            src_ref=src, dst_ref=dst, send_sem=send, recv_sem=recv,
            device_id=target, device_id_type=MESH,
        )

    def members_of(c, shift):
        return pl.ds(pl.multiple_of(((c + shift * heavy) % chunks) * MC, MC), MC)

    def columns_of(m):
        return pl.ds(pl.multiple_of(m * cols, cols), cols)

    def send2(c):
        return remote(
            anom.at[:, members_of(c, odd), :], r2.at[:, members_of(c, 0), :],
            s2.at[c], q2.at[c], at(-2 * sign, 0),
        )

    def send3(m):
        return remote(
            anom.at[:, members_of(last, odd), columns_of(m)],
            r2.at[:, members_of(last, 0), columns_of(m)],
            s3.at[m], q3.at[m], at(-2 * sign, 0),
        )

    def send1(c):
        return remote(
            anom.at[:, members_of(c, 1 - odd), :], r1.at[:, members_of(c, 0), :],
            s1.at[c], q1.at[c], at(sign, 0),
        )

    def relay():
        return remote(
            r1.at[:, members_of(heavy - 1, 0), columns_of(0)],
            r2.at[:, members_of(last, 0), columns_of(0)],
            relay_s, q3.at[0], at(-3, 0),
        )

    def to(u):
        return sign if u == 1 else -2 * sign

    def send_tab(u):
        return remote(near_far.at[u - 1], tab_in.at[u - 1], tab_s.at[u - 1], tab_r.at[u - 1], at(to(u), 0))

    def send_innov(u):
        where = columns_of(me) if u == 2 else pl.ds(0, width)
        return remote(
            innov.at[:, where], innov_in.at[u - 1, :, where], in_s.at[u - 1], in_r.at[u - 1], at(to(u), 0)
        )

    def share_innov(k, owner):
        where = columns_of(owner)
        return remote(
            innov_in.at[1, :, where], innov_in.at[1, :, where], fs.at[k], fr.at[k], at(0, k)
        )

    def send_part(u, m):
        return remote(
            part.at[u, m], got.at[u, me], ps.at[u, m], pr.at[u, me],
            ((d + (0, sign, 2 * sign)[u] + states) % states, m),
        )

    def part_from(u, m):
        return remote(part.at[u, m], got.at[u, m], ps.at[u, m], pr.at[u, m], at(sign, 0))

    pl.semaphore_wait(barrier, len(greeted))
    send2(0).start()
    send1(0).start()
    for load in (load_n, load_x, load_p, load_c, load_v, load_a, load_t):
        load.start()
    acc[...] = jnp.zeros_like(acc)

    load_n.wait()
    load_x.wait()
    load_p.wait()
    row = lax.broadcasted_iota(jnp.int32, (blocks, slots), 0)
    slot = lax.broadcasted_iota(jnp.int32, (blocks, slots), 1)
    count = jnp.zeros((blocks, slots), jnp.int32)
    for i in range(blocks):
        count = jnp.where(row == i, cnt[i], count)
    valid = slot < count
    block = nbr[...]
    home = lax.div(block, jnp.int32(blocks))
    base = tix[...] * (3 * blocks) + block - home * blocks
    gap = home - d
    gap = jnp.where(gap > HOPS, gap - states, jnp.where(gap < -HOPS, gap + states, gap)) * sign
    near = jnp.where(gap == 1, base, jnp.where(gap == -1, base + 2 * blocks, none))
    far = jnp.where(gap == -2, base, jnp.where(gap == -1, base + blocks, none))
    near_far[...] = jnp.full(near_far.shape, none, jnp.int32)
    local[...] = jnp.full(local.shape, none, jnp.int32)
    near_far[0, :, 0:slots] = jnp.where(valid, near, none)
    near_far[1, :, 0:slots] = jnp.where(valid, far, none)
    local[0, :, 0:slots] = jnp.where(valid & (gap >= 0), base + gap * blocks, none)
    local[1, :, 0:slots] = jnp.where(valid & (gap == 0), base, none)
    local[2, :, 0:slots] = jnp.where(valid & (gap == 2), base + 2 * blocks, none)
    load_tab = pltpu.make_async_copy(local, tab0, obs_s.at[5])
    load_tab.start()
    for u in (1, 2):
        send_tab(u).start()

    def hot_row(k, carry):
        cell = cells[pl.ds(k, 1), :]
        value = values[pl.ds(k, 1), :]
        lo = cell & (LANES - 1)
        block = cell // width
        group = (cell // LANES) % groups
        hi = group * blocks + block
        v1 = value.astype(jnp.bfloat16).astype(jnp.float32)
        rest = value - v1
        v2 = rest.astype(jnp.bfloat16).astype(jnp.float32)
        v3 = rest - v2
        rows = blocks * groups
        same = lax.broadcasted_iota(jnp.int32, (rows, LANES), 0) == hi
        where = pl.ds(pl.multiple_of(k * LANES, LANES), LANES)
        for n, v in enumerate((v1, v2, v3)):
            hot[pl.ds(n * rows, rows), where] = jnp.where(
                same, jnp.broadcast_to(v, (rows, LANES)), 0.0
            ).astype(jnp.bfloat16)
        low[:, where] = jnp.where(
            lax.broadcasted_iota(jnp.int32, (LANES, LANES), 0) == lo, 1.0, 0.0
        ).astype(jnp.bfloat16)
        return carry

    load_c.wait()
    load_v.wait()
    lax.fori_loop(0, cells.shape[0], hot_row, 0)
    rows = blocks * groups
    sums = lax.dot_general(
        hot[...], low[...], (((1,), (1,)), ((), ())), preferred_element_type=jnp.float32
    )
    total = sums[0:rows] + sums[rows : 2 * rows] + sums[2 * rows : 3 * rows]
    for g in range(groups):
        innov[:, g * LANES : (g + 1) * LANES] = total[g * blocks : (g + 1) * blocks]
    for u in (1, 2):
        send_innov(u).start()
    for c in range(1, last):
        send2(c).start()

    @pl.when(d > 1)
    def _():
        send3(0).start()

    @pl.when(d != 1)
    def _():
        for m in range(1, members - 1):
            send3(m).start()

    @pl.when((d != 1) & (d != states - 2))
    def _():
        send3(members - 1).start()

    for c in range(1, heavy):
        send1(c).start()

    load_a.wait()
    for c in range(chunks):
        for j in range(blocks):
            own_w[c, j] = (
                av[j, members_of(c, odd), :].astype(jnp.float32) * innov[pl.ds(j, 1), :]
            ).astype(jnp.bfloat16)
    load_t.wait()

    def own_z(t, carry):
        res = lax.dot_general(
            own_w[...].reshape(chunks * blocks * MC, width), tv[t],
            (((1,), (1,)), ((), ())), preferred_element_type=jnp.float32,
        )
        z[:, pl.ds(t * 3 * blocks, blocks)] = res.reshape(chunks, blocks, MC, width)
        return carry

    lax.fori_loop(0, KT, own_z, 0)
    for c in range(heavy, chunks):
        for t in range(KT):
            z[c, (t * 3 + 1) * blocks : (t * 3 + 2) * blocks] = jnp.zeros((blocks, MC, width), jnp.float32)
    for c in range(chunks):
        z[c, none] = jnp.zeros((MC, width), jnp.float32)

    send_innov(2).wait_recv()
    for k in range(1, members):
        share_innov(k, me).start()

    load_tab.wait()
    for u in (1, 2):
        send_tab(u).wait_recv()
        fill = pltpu.make_async_copy(tab_in.at[u - 1], idx.at[u - 1], idx_s.at[u - 1])
        fill.start()
        fill.wait()

    def offset_slot(g):
        return {-2: 1 + 3 * odd, -1: 2 + odd, 1: 3 - odd, 2: 4 - 3 * odd}[g]

    free = list(range(fixed, slots))

    def spread(c, table, i, named):
        total = z[c, table(i, named[0])]
        for s in named[1:] + free:
            total = total + z[c, table(i, s)]
        return total

    def pairs(c, u, table, named, source, shift):
        def one(i, carry):
            value = source[i, members_of(c, shift), :].astype(jnp.float32) * spread(c, table, i, named)
            acc[u, i] += jnp.sum(value.reshape(MC // 8, 8, width), axis=0)
            return carry

        lax.fori_loop(0, blocks, one, 0)

    def table0(k):
        return lambda i, s: tab0[k, i, s]

    def table_in(u):
        return lambda i, s: idx[u - 1, i, s]

    def fold(u):
        for i in range(blocks):
            line = jnp.sum(acc[u, i], axis=0, keepdims=True)
            for m in range(members):
                part[u, m, i : i + 1, :] = line[:, m * cols : (m + 1) * cols]

    def far_z(c, first):
        for g, r in enumerate((r1, r2)):
            if g or not first:
                for j in range(blocks):
                    wr[g * blocks + j] = (
                        r[j, members_of(c, 0), :].astype(jnp.float32)
                        * innov_in[g, pl.ds(j, 1), :]
                    ).astype(jnp.bfloat16)
        count = 2 * blocks - first

        def one(t, carry):
            res = lax.dot_general(
                wr[pl.ds(first, count)].reshape(count * MC, width), tv[t],
                (((1,), (1,)), ((), ())), preferred_element_type=jnp.float32,
            )
            z[c, pl.ds(t * 3 * blocks + blocks + first, count)] = res.reshape(count, MC, width)
            return carry

        lax.fori_loop(0, KT, one, 0)

    def full_step(c, carry):
        send2(c).wait_recv()
        send1(c).wait_recv()

        @pl.when((c == heavy - 1) & (d == 1))
        def _():
            relay().start()
            for m in range(members):
                send3(m).start()

        @pl.when(c == 0)
        def _():
            for k in range(1, members):
                pl.semaphore_signal(peers, inc=1, device_id=at(0, k), device_id_type=MESH)

        far_z(c, 0)
        pairs(c, 2, table_in(2), [offset_slot(-2), offset_slot(-1)], r2, 0)
        pairs(c, 1, table_in(1), [offset_slot(-1), offset_slot(1)], r1, 0)
        pairs(c, 0, table0(0), [0, offset_slot(1), offset_slot(2)], av, odd)
        return carry

    def ahead(c, carry):
        def one(i, carry):
            v2[c - heavy, i] = spread(c, table_in(2), i, [offset_slot(-2)])
            return carry

        lax.fori_loop(0, blocks, one, 0)
        pairs(c, 0, table0(1), [0], av, odd)
        return carry

    lax.fori_loop(heavy, chunks, ahead, 0)
    send_innov(1).wait_recv()
    for k in range(1, members):
        share_innov(k, (me + members - k) % members).wait_recv()
    lax.fori_loop(0, heavy, full_step, 0)
    fold(1)
    pl.semaphore_wait(peers, members - 1)
    for m in range(members):
        send_part(1, m).start()

    def reach(c):
        def one(i, carry):
            value = r2[i, members_of(c, 0), :].astype(jnp.float32) * v2[c - heavy, i]
            acc[2, i] += jnp.sum(value.reshape(MC // 8, 8, width), axis=0)
            return carry

        lax.fori_loop(0, blocks, one, 0)

    def fold_columns(u, m, i, value):
        where = columns_of(m)
        line = acc[u, i, :, where] + jnp.sum(value.reshape(MC // 8, 8, cols), axis=0)
        part[u, m, i : i + 1, :] = jnp.sum(line, axis=0, keepdims=True)

    def reach_columns(m):
        where = slice(m * cols, (m + 1) * cols)
        send3(m).wait_recv()
        for i in range(blocks):
            fold_columns(
                2, m, i,
                r2[i, members_of(last, 0), where].astype(jnp.float32) * v2[last - heavy, i, :, where],
            )
        send_part(2, m).start()

    def light_step(c, carry):
        send2(c).wait_recv()
        reach(c)

        @pl.when((d == states - 2) & (c == last - 1))
        def _():
            reach_columns(0)
            send3(members - 1).start()

        far_z(c, blocks)
        return carry

    lax.fori_loop(heavy, last, light_step, 0)

    def depth_z(m, t, where):
        inner = slice(m * cols, (m + 1) * cols)
        res = lax.dot_general(
            wr[blocks : 2 * blocks, :, inner].reshape(blocks * MC, cols), tv[t, where, inner],
            (((1,), (1,)), ((), ())), preferred_element_type=jnp.float32,
        ).reshape(blocks, MC, -1)
        panels = slice((t * 3 + 2) * blocks, (t * 3 + 3) * blocks)
        if m:
            res = z[last, panels, :, where] + res
        z[last, panels, :, where] = res

    for m in range(members):
        where = slice(m * cols, (m + 1) * cols)
        if m:
            reach_columns(m)
        else:
            @pl.when(d != states - 2)
            def _():
                reach_columns(0)

        for j in range(blocks):
            wr[blocks + j, :, where] = (
                r2[j, members_of(last, 0), where].astype(jnp.float32) * innov_in[1, pl.ds(j, 1), where]
            ).astype(jnp.bfloat16)
        if m < members - 1:
            for t in range(KT):
                depth_z(m, t, pl.ds(0, width))
        if m == members - 2:
            for c in range(heavy, last):
                pairs(c, 0, table0(2), [offset_slot(2)], av, odd)

    chips = members // CORES
    for away in range(members - 1, -1, -1):
        m = (me // CORES + away // CORES) % chips * CORES + (me + away) % CORES
        where = columns_of(m)
        for t in range(KT):
            depth_z(members - 1, t, where)
        for i in range(blocks):
            total = z[last, tab0[2, i, offset_slot(2)], :, where]
            for s in free:
                total = total + z[last, tab0[2, i, s], :, where]
            fold_columns(0, m, i, av[i, members_of(last, odd), where].astype(jnp.float32) * total)
        if away:
            send_part(0, m).start()
    for u in (1, 2):
        send_tab(u).wait_send()
        send_innov(u).wait_send()
    for c in range(last):
        send2(c).wait_send()
    for m in range(1, members):
        send3(m).wait_send()

    @pl.when(d > 0)
    def _():
        send3(0).wait_send()

    @pl.when(d == 1)
    def _():
        relay().wait_send()

    for k in range(1, members):
        share_innov(k, me).wait_send()
    for c in range(heavy):
        send1(c).wait_send()
    for u in (1, 2):
        for m in range(members):
            send_part(u, m).wait_send()
    total = part[0, me]
    for u in (1, 2):
        for m in range(members):
            part_from(u, m).wait_recv()
            total = total + got[u, m]
    for k in range(1, members):
        m = (me + k) % members
        part_from(0, m).wait_recv()
        total = total + got[0, m]
    out[...] = total / jnp.float32(M - 1)
    for k in range(1, members):
        send_part(0, (me + k) % members).wait_send()


def on_device(states, members, anomalies, tapers, nbr_block, taper_index, pair_count, obs_cell, obs_value):
    blocks, mem, width = anomalies.shape
    slots = nbr_block.shape[1]
    chunks = mem // MC
    cols = width // members
    cells = obs_cell.reshape(-1, LANES)
    values = obs_value.reshape(-1, LANES)
    rows = blocks * (width // LANES)
    dma = pltpu.SemaphoreType.DMA
    any_space = pl.BlockSpec(memory_space=pl.ANY)
    vmem = pl.BlockSpec(memory_space=pltpu.VMEM)
    return pl.pallas_call(
        functools.partial(kernel, states, members, slots),
        out_shape=pltpu.VMEM((blocks, cols), jnp.float32),
        in_specs=[any_space] * 7,
        out_specs=vmem,
        scratch_shapes=[
            pltpu.VMEM(nbr_block.shape, jnp.int32),
            pltpu.VMEM(taper_index.shape, jnp.int32),
            pltpu.SMEM(pair_count.shape, jnp.int32),
            pltpu.VMEM((2, blocks, LANES), jnp.int32),
            pltpu.VMEM((3, blocks, LANES), jnp.int32),
            pltpu.SMEM((3, blocks, LANES), jnp.int32),
            pltpu.VMEM(cells.shape, jnp.int32),
            pltpu.VMEM(values.shape, jnp.float32),
            dma((6,)),
            pltpu.VMEM((blocks, mem, width), jnp.bfloat16),
            pltpu.VMEM(tapers.shape, jnp.bfloat16),
            pltpu.VMEM((blocks, mem, width), jnp.bfloat16),
            pltpu.VMEM((blocks, mem, width), jnp.bfloat16),
            pltpu.VMEM((2, blocks, LANES), jnp.int32),
            pltpu.SMEM((2, blocks, LANES), jnp.int32),
            pltpu.VMEM((blocks, width), jnp.float32),
            pltpu.VMEM((2, blocks, width), jnp.float32),
            pltpu.VMEM((3 * rows, obs_cell.shape[0]), jnp.bfloat16),
            pltpu.VMEM((LANES, obs_cell.shape[0]), jnp.bfloat16),
            pltpu.VMEM((chunks, KT * 3 * blocks + 1, MC, width), jnp.float32),
            pltpu.VMEM((chunks, blocks, MC, width), jnp.bfloat16),
            pltpu.VMEM((2 * blocks, MC, width), jnp.bfloat16),
            pltpu.VMEM((chunks // 2, blocks, MC, width), jnp.float32),
            pltpu.VMEM((3, blocks, 8, width), jnp.float32),
            pltpu.VMEM((3, members, blocks, cols), jnp.float32),
            pltpu.VMEM((3, members, blocks, cols), jnp.float32),
            dma((2,)), dma((2,)), dma((2,)), dma, dma,
            dma((chunks,)), dma((chunks,)),
            dma((chunks,)), dma((chunks,)),
            dma((members,)), dma((members,)), dma,
            dma((2,)), dma((2,)),
            dma((members,)), dma((members,)),
            dma((3, members)), dma((3, members)),
            pltpu.SemaphoreType.REGULAR,
        ],
        compiler_params=pltpu.CompilerParams(
            collective_id=0, has_side_effects=True, vmem_limit_bytes=66_000_000
        ),
    )(nbr_block, taper_index, pair_count, cells, values, anomalies, tapers)


def solution(mesh):
    placed = (
        P("state", "member", None),
        P(),
        P("state", None),
        P("state", None),
        P("state"),
        P("state"),
        P("state"),
    )
    return jax.shard_map(
        functools.partial(on_device, mesh.shape["state"], mesh.shape["member"]),
        mesh=mesh, in_specs=placed, out_specs=P("state", "member"), check_vma=False,
    )
```

```python
import functools

import jax
import jax.numpy as jnp
from jax import lax
from jax.experimental import pallas as pl
from jax.experimental.pallas import tpu as pltpu
from jax.sharding import PartitionSpec as P

M = 256
HOPS = 2
KT = 2
LANES = 128
MC = 16
CORES = 2
MESH = pl.DeviceIdType.MESH


def kernel(
    states, members, slots,
    nbr_hbm, tix_hbm, cnt_hbm, cells_hbm, values_hbm, anom, tapers, out,
    nbr, tix, cnt, near_far, local, tab0, cells, values, obs_s, av, tv, r1, r2, tab_in, idx, innov, innov_in,
    hot, low, z, own_w, wr, v2, acc, part, got,
    tab_s, tab_r, idx_s, av_s, tv_s, s1, q1, s2, q2, s3, q3, relay_s, in_s, in_r, fs, fr, ps, pr, peers, entered,
):
    blocks, mem, width = anom.shape
    chunks = mem // MC
    last = chunks - 1
    groups = width // LANES
    cols = width // members
    none = KT * 3 * blocks
    d = lax.axis_index("state")
    me = lax.axis_index("member")
    odd = d % 2
    sign = 1 - 2 * odd
    heavy = chunks // 2
    fixed = 2 * HOPS + 1

    def at(ds, dm):
        return ((d + ds + states) % states, (me + dm) % members)

    barrier = pltpu.get_barrier_semaphore()
    greeted = [(sign, 0), (2 * sign, 0)]
    for ds, dm in greeted:
        pl.semaphore_signal(barrier, inc=1, device_id=at(ds, dm), device_id_type=MESH)

    @pl.when(d != states - 1)
    def _():
        for k in range(1, members):
            pl.semaphore_signal(barrier, inc=1, device_id=at(0, k), device_id_type=MESH)

    load_n = pltpu.make_async_copy(nbr_hbm, nbr, obs_s.at[2])
    load_x = pltpu.make_async_copy(tix_hbm, tix, obs_s.at[3])
    load_p = pltpu.make_async_copy(cnt_hbm, cnt, obs_s.at[4])
    load_a = pltpu.make_async_copy(anom, av, av_s)
    load_t = pltpu.make_async_copy(tapers, tv, tv_s)
    load_c = pltpu.make_async_copy(cells_hbm, cells, obs_s.at[0])
    load_v = pltpu.make_async_copy(values_hbm, values, obs_s.at[1])

    def remote(src, dst, send, recv, target):
        return pltpu.make_async_remote_copy(
            src_ref=src, dst_ref=dst, send_sem=send, recv_sem=recv,
            device_id=target, device_id_type=MESH,
        )

    def members_of(c, shift):
        return pl.ds(pl.multiple_of(((c + shift * heavy) % chunks) * MC, MC), MC)

    def columns_of(m):
        return pl.ds(pl.multiple_of(m * cols, cols), cols)

    def send2(c):
        return remote(
            anom.at[:, members_of(c, odd), :], r2.at[:, members_of(c, 0), :],
            s2.at[c], q2.at[c], at(-2 * sign, 0),
        )

    def send3(m):
        return remote(
            anom.at[:, members_of(last, odd), columns_of(m)],
            r2.at[:, members_of(last, 0), columns_of(m)],
            s3.at[m], q3.at[m], at(-2 * sign, 0),
        )

    def send1(c):
        return remote(
            anom.at[:, members_of(c, 1 - odd), :], r1.at[:, members_of(c, 0), :],
            s1.at[c], q1.at[c], at(sign, 0),
        )

    def relay():
        return remote(
            r1.at[:, members_of(heavy - 1, 0), columns_of(0)],
            r2.at[:, members_of(last, 0), columns_of(0)],
            relay_s, q3.at[0], at(-3, 0),
        )

    def to(u):
        return sign if u == 1 else -2 * sign

    def send_tab(u):
        return remote(near_far.at[u - 1], tab_in.at[u - 1], tab_s.at[u - 1], tab_r.at[u - 1], at(to(u), 0))

    def send_innov(u):
        where = columns_of(me) if u == 2 else pl.ds(0, width)
        return remote(
            innov.at[:, where], innov_in.at[u - 1, :, where], in_s.at[u - 1], in_r.at[u - 1], at(to(u), 0)
        )

    def share_innov(k, owner):
        where = columns_of(owner)
        return remote(
            innov_in.at[1, :, where], innov_in.at[1, :, where], fs.at[k], fr.at[k], at(0, k)
        )

    def send_part(u, m):
        return remote(
            part.at[u, m], got.at[u, me], ps.at[u, m], pr.at[u, me],
            ((d + (0, sign, 2 * sign)[u] + states) % states, m),
        )

    def part_from(u, m):
        return remote(part.at[u, m], got.at[u, m], ps.at[u, m], pr.at[u, m], at(sign, 0))

    pl.semaphore_wait(barrier, jnp.where(d == states - 1, len(greeted), len(greeted) + members - 1))
    send2(0).start()
    send1(0).start()
    for load in (load_n, load_x, load_p, load_c, load_v, load_a, load_t):
        load.start()
    acc[...] = jnp.zeros_like(acc)

    load_n.wait()
    load_x.wait()
    load_p.wait()
    row = lax.broadcasted_iota(jnp.int32, (blocks, slots), 0)
    slot = lax.broadcasted_iota(jnp.int32, (blocks, slots), 1)
    count = jnp.zeros((blocks, slots), jnp.int32)
    for i in range(blocks):
        count = jnp.where(row == i, cnt[i], count)
    valid = slot < count
    block = nbr[...]
    home = lax.div(block, jnp.int32(blocks))
    base = tix[...] * (3 * blocks) + block - home * blocks
    gap = home - d
    gap = jnp.where(gap > HOPS, gap - states, jnp.where(gap < -HOPS, gap + states, gap)) * sign
    near = jnp.where(gap == 1, base, jnp.where(gap == -1, base + 2 * blocks, none))
    far = jnp.where(gap == -2, base, jnp.where(gap == -1, base + blocks, none))
    near_far[...] = jnp.full(near_far.shape, none, jnp.int32)
    local[...] = jnp.full(local.shape, none, jnp.int32)
    near_far[0, :, 0:slots] = jnp.where(valid, near, none)
    near_far[1, :, 0:slots] = jnp.where(valid, far, none)
    local[0, :, 0:slots] = jnp.where(valid & (gap >= 0), base + gap * blocks, none)
    local[1, :, 0:slots] = jnp.where(valid & (gap == 0), base, none)
    local[2, :, 0:slots] = jnp.where(valid & (gap == 2), base + 2 * blocks, none)
    load_tab = pltpu.make_async_copy(local, tab0, obs_s.at[5])
    load_tab.start()
    for u in (1, 2):
        send_tab(u).start()

    @pl.when(d == states - 2)
    def _():
        for k in range(1, members):
            pl.semaphore_signal(entered, inc=1, device_id=at(0, k), device_id_type=MESH)
        pl.semaphore_wait(entered, members - 1)
        pl.semaphore_signal(entered, inc=1, device_id=at(sign, 0), device_id_type=MESH)

    def hot_row(k, carry):
        cell = cells[pl.ds(k, 1), :]
        value = values[pl.ds(k, 1), :]
        lo = cell & (LANES - 1)
        block = cell // width
        group = (cell // LANES) % groups
        hi = group * blocks + block
        v1 = value.astype(jnp.bfloat16).astype(jnp.float32)
        rest = value - v1
        v2 = rest.astype(jnp.bfloat16).astype(jnp.float32)
        v3 = rest - v2
        rows = blocks * groups
        same = lax.broadcasted_iota(jnp.int32, (rows, LANES), 0) == hi
        where = pl.ds(pl.multiple_of(k * LANES, LANES), LANES)
        for n, v in enumerate((v1, v2, v3)):
            hot[pl.ds(n * rows, rows), where] = jnp.where(
                same, jnp.broadcast_to(v, (rows, LANES)), 0.0
            ).astype(jnp.bfloat16)
        low[:, where] = jnp.where(
            lax.broadcasted_iota(jnp.int32, (LANES, LANES), 0) == lo, 1.0, 0.0
        ).astype(jnp.bfloat16)
        return carry

    load_c.wait()
    load_v.wait()
    lax.fori_loop(0, cells.shape[0], hot_row, 0)
    rows = blocks * groups
    sums = lax.dot_general(
        hot[...], low[...], (((1,), (1,)), ((), ())), preferred_element_type=jnp.float32
    )
    total = sums[0:rows] + sums[rows : 2 * rows] + sums[2 * rows : 3 * rows]
    for g in range(groups):
        innov[:, g * LANES : (g + 1) * LANES] = total[g * blocks : (g + 1) * blocks]
    for u in (1, 2):
        send_innov(u).start()
    for c in range(1, last):
        send2(c).start()

    @pl.when(d > 1)
    def _():
        send3(0).start()

    @pl.when(d != 1)
    def _():
        for m in range(1, members - 1):
            send3(m).start()

    @pl.when((d != 1) & (d != states - 2))
    def _():
        send3(members - 1).start()

    for c in range(1, heavy):
        send1(c).start()

    load_a.wait()
    for c in range(chunks):
        for j in range(blocks):
            own_w[c, j] = (
                av[j, members_of(c, odd), :].astype(jnp.float32) * innov[pl.ds(j, 1), :]
            ).astype(jnp.bfloat16)
    load_t.wait()

    def own_z(t, carry):
        res = lax.dot_general(
            own_w[...].reshape(chunks * blocks * MC, width), tv[t],
            (((1,), (1,)), ((), ())), preferred_element_type=jnp.float32,
        )
        z[:, pl.ds(t * 3 * blocks, blocks)] = res.reshape(chunks, blocks, MC, width)
        return carry

    lax.fori_loop(0, KT, own_z, 0)
    for c in range(heavy, chunks):
        for t in range(KT):
            z[c, (t * 3 + 1) * blocks : (t * 3 + 2) * blocks] = jnp.zeros((blocks, MC, width), jnp.float32)
    for c in range(chunks):
        z[c, none] = jnp.zeros((MC, width), jnp.float32)

    send_innov(2).wait_recv()

    @pl.when(d == states - 1)
    def _():
        pl.semaphore_wait(entered, 1)

    for k in range(1, members):
        share_innov(k, me).start()

    load_tab.wait()
    for u in (1, 2):
        send_tab(u).wait_recv()
        fill = pltpu.make_async_copy(tab_in.at[u - 1], idx.at[u - 1], idx_s.at[u - 1])
        fill.start()
        fill.wait()

    def offset_slot(g):
        return {-2: 1 + 3 * odd, -1: 2 + odd, 1: 3 - odd, 2: 4 - 3 * odd}[g]

    free = list(range(fixed, slots))

    def spread(c, table, i, named):
        total = z[c, table(i, named[0])]
        for s in named[1:] + free:
            total = total + z[c, table(i, s)]
        return total

    def pairs(c, u, table, named, source, shift):
        def one(i, carry):
            value = source[i, members_of(c, shift), :].astype(jnp.float32) * spread(c, table, i, named)
            acc[u, i] += jnp.sum(value.reshape(MC // 8, 8, width), axis=0)
            return carry

        lax.fori_loop(0, blocks, one, 0)

    def table0(k):
        return lambda i, s: tab0[k, i, s]

    def table_in(u):
        return lambda i, s: idx[u - 1, i, s]

    def fold(u):
        for i in range(blocks):
            line = jnp.sum(acc[u, i], axis=0, keepdims=True)
            for m in range(members):
                part[u, m, i : i + 1, :] = line[:, m * cols : (m + 1) * cols]

    def far_z(c, first):
        for g, r in enumerate((r1, r2)):
            if g or not first:
                for j in range(blocks):
                    wr[g * blocks + j] = (
                        r[j, members_of(c, 0), :].astype(jnp.float32)
                        * innov_in[g, pl.ds(j, 1), :]
                    ).astype(jnp.bfloat16)
        count = 2 * blocks - first

        def one(t, carry):
            res = lax.dot_general(
                wr[pl.ds(first, count)].reshape(count * MC, width), tv[t],
                (((1,), (1,)), ((), ())), preferred_element_type=jnp.float32,
            )
            z[c, pl.ds(t * 3 * blocks + blocks + first, count)] = res.reshape(count, MC, width)
            return carry

        lax.fori_loop(0, KT, one, 0)

    def full_step(c, carry):
        send2(c).wait_recv()
        send1(c).wait_recv()

        @pl.when((c == heavy - 1) & (d == 1))
        def _():
            relay().start()
            for m in range(members):
                send3(m).start()

        @pl.when(c == 0)
        def _():
            for k in range(1, members):
                pl.semaphore_signal(peers, inc=1, device_id=at(0, k), device_id_type=MESH)

        far_z(c, 0)
        pairs(c, 2, table_in(2), [offset_slot(-2), offset_slot(-1)], r2, 0)
        pairs(c, 1, table_in(1), [offset_slot(-1), offset_slot(1)], r1, 0)
        pairs(c, 0, table0(0), [0, offset_slot(1), offset_slot(2)], av, odd)
        return carry

    def ahead(c, carry):
        def one(i, carry):
            v2[c - heavy, i] = spread(c, table_in(2), i, [offset_slot(-2)])
            return carry

        lax.fori_loop(0, blocks, one, 0)
        pairs(c, 0, table0(1), [0], av, odd)
        return carry

    lax.fori_loop(heavy, chunks, ahead, 0)
    send_innov(1).wait_recv()
    for k in range(1, members):
        share_innov(k, (me + members - k) % members).wait_recv()
    lax.fori_loop(0, heavy, full_step, 0)
    fold(1)
    pl.semaphore_wait(peers, members - 1)
    for m in range(members):
        send_part(1, m).start()

    def reach(c):
        def one(i, carry):
            value = r2[i, members_of(c, 0), :].astype(jnp.float32) * v2[c - heavy, i]
            acc[2, i] += jnp.sum(value.reshape(MC // 8, 8, width), axis=0)
            return carry

        lax.fori_loop(0, blocks, one, 0)

    def fold_columns(u, m, i, value):
        where = columns_of(m)
        line = acc[u, i, :, where] + jnp.sum(value.reshape(MC // 8, 8, cols), axis=0)
        part[u, m, i : i + 1, :] = jnp.sum(line, axis=0, keepdims=True)

    def reach_columns(m):
        where = slice(m * cols, (m + 1) * cols)
        send3(m).wait_recv()
        for i in range(blocks):
            fold_columns(
                2, m, i,
                r2[i, members_of(last, 0), where].astype(jnp.float32) * v2[last - heavy, i, :, where],
            )
        send_part(2, m).start()

    def light_step(c, carry):
        send2(c).wait_recv()
        reach(c)

        @pl.when((d == states - 2) & (c == last - 1))
        def _():
            reach_columns(0)
            send3(members - 1).start()
            reach_columns(1)

        far_z(c, blocks)
        return carry

    lax.fori_loop(heavy, last, light_step, 0)

    def depth_z(m, t, where):
        inner = slice(m * cols, (m + 1) * cols)
        res = lax.dot_general(
            wr[blocks : 2 * blocks, :, inner].reshape(blocks * MC, cols), tv[t, where, inner],
            (((1,), (1,)), ((), ())), preferred_element_type=jnp.float32,
        ).reshape(blocks, MC, -1)
        panels = slice((t * 3 + 2) * blocks, (t * 3 + 3) * blocks)
        if m:
            res = z[last, panels, :, where] + res
        z[last, panels, :, where] = res

    for m in range(members):
        where = slice(m * cols, (m + 1) * cols)

        @pl.when(d != states - 2)
        def _():
            reach_columns(m)

        if m + 2 < members:
            @pl.when(d == states - 2)
            def _():
                reach_columns(m + 2)

        for j in range(blocks):
            wr[blocks + j, :, where] = (
                r2[j, members_of(last, 0), where].astype(jnp.float32) * innov_in[1, pl.ds(j, 1), where]
            ).astype(jnp.bfloat16)
        if m < members - 1:
            for t in range(KT):
                depth_z(m, t, pl.ds(0, width))
        if m == members - 2:
            for c in range(heavy, last):
                pairs(c, 0, table0(2), [offset_slot(2)], av, odd)

    chips = members // CORES
    for away in range(members - 1, -1, -1):
        m = (me // CORES + away // CORES) % chips * CORES + (me + away) % CORES
        where = columns_of(m)
        for t in range(KT):
            depth_z(members - 1, t, where)
        for i in range(blocks):
            total = z[last, tab0[2, i, offset_slot(2)], :, where]
            for s in free:
                total = total + z[last, tab0[2, i, s], :, where]
            fold_columns(0, m, i, av[i, members_of(last, odd), where].astype(jnp.float32) * total)
        if away:
            send_part(0, m).start()
    for u in (1, 2):
        send_tab(u).wait_send()
        send_innov(u).wait_send()
    for c in range(last):
        send2(c).wait_send()
    for m in range(1, members):
        send3(m).wait_send()

    @pl.when(d > 0)
    def _():
        send3(0).wait_send()

    @pl.when(d == 1)
    def _():
        relay().wait_send()

    for k in range(1, members):
        share_innov(k, me).wait_send()
    for c in range(heavy):
        send1(c).wait_send()
    for u in (1, 2):
        for m in range(members):
            send_part(u, m).wait_send()
    total = part[0, me]
    for u in (1, 2):
        for m in range(members):
            part_from(u, m).wait_recv()
            total = total + got[u, m]
    for k in range(1, members):
        m = (me + k) % members
        part_from(0, m).wait_recv()
        total = total + got[0, m]
    out[...] = total / jnp.float32(M - 1)
    for k in range(1, members):
        send_part(0, (me + k) % members).wait_send()


def on_device(states, members, anomalies, tapers, nbr_block, taper_index, pair_count, obs_cell, obs_value):
    blocks, mem, width = anomalies.shape
    slots = nbr_block.shape[1]
    chunks = mem // MC
    cols = width // members
    cells = obs_cell.reshape(-1, LANES)
    values = obs_value.reshape(-1, LANES)
    rows = blocks * (width // LANES)
    dma = pltpu.SemaphoreType.DMA
    any_space = pl.BlockSpec(memory_space=pl.ANY)
    vmem = pl.BlockSpec(memory_space=pltpu.VMEM)
    return pl.pallas_call(
        functools.partial(kernel, states, members, slots),
        out_shape=pltpu.VMEM((blocks, cols), jnp.float32),
        in_specs=[any_space] * 7,
        out_specs=vmem,
        scratch_shapes=[
            pltpu.VMEM(nbr_block.shape, jnp.int32),
            pltpu.VMEM(taper_index.shape, jnp.int32),
            pltpu.SMEM(pair_count.shape, jnp.int32),
            pltpu.VMEM((2, blocks, LANES), jnp.int32),
            pltpu.VMEM((3, blocks, LANES), jnp.int32),
            pltpu.SMEM((3, blocks, LANES), jnp.int32),
            pltpu.VMEM(cells.shape, jnp.int32),
            pltpu.VMEM(values.shape, jnp.float32),
            dma((6,)),
            pltpu.VMEM((blocks, mem, width), jnp.bfloat16),
            pltpu.VMEM(tapers.shape, jnp.bfloat16),
            pltpu.VMEM((blocks, mem, width), jnp.bfloat16),
            pltpu.VMEM((blocks, mem, width), jnp.bfloat16),
            pltpu.VMEM((2, blocks, LANES), jnp.int32),
            pltpu.SMEM((2, blocks, LANES), jnp.int32),
            pltpu.VMEM((blocks, width), jnp.float32),
            pltpu.VMEM((2, blocks, width), jnp.float32),
            pltpu.VMEM((3 * rows, obs_cell.shape[0]), jnp.bfloat16),
            pltpu.VMEM((LANES, obs_cell.shape[0]), jnp.bfloat16),
            pltpu.VMEM((chunks, KT * 3 * blocks + 1, MC, width), jnp.float32),
            pltpu.VMEM((chunks, blocks, MC, width), jnp.bfloat16),
            pltpu.VMEM((2 * blocks, MC, width), jnp.bfloat16),
            pltpu.VMEM((chunks // 2, blocks, MC, width), jnp.float32),
            pltpu.VMEM((3, blocks, 8, width), jnp.float32),
            pltpu.VMEM((3, members, blocks, cols), jnp.float32),
            pltpu.VMEM((3, members, blocks, cols), jnp.float32),
            dma((2,)), dma((2,)), dma((2,)), dma, dma,
            dma((chunks,)), dma((chunks,)),
            dma((chunks,)), dma((chunks,)),
            dma((members,)), dma((members,)), dma,
            dma((2,)), dma((2,)),
            dma((members,)), dma((members,)),
            dma((3, members)), dma((3, members)),
            pltpu.SemaphoreType.REGULAR,
            pltpu.SemaphoreType.REGULAR,
        ],
        compiler_params=pltpu.CompilerParams(
            collective_id=0, has_side_effects=True, vmem_limit_bytes=66_000_000
        ),
    )(nbr_block, taper_index, pair_count, cells, values, anomalies, tapers)


def solution(mesh):
    placed = (
        P("state", "member", None),
        P(),
        P("state", None),
        P("state", None),
        P("state"),
        P("state"),
        P("state"),
    )
    return jax.shard_map(
        functools.partial(on_device, mesh.shape["state"], mesh.shape["member"]),
        mesh=mesh, in_specs=placed, out_specs=P("state", "member"), check_vma=False,
    )
```

```python
import functools

import jax
import jax.numpy as jnp
from jax import lax
from jax.experimental import pallas as pl
from jax.experimental.pallas import tpu as pltpu
from jax.sharding import PartitionSpec as P

M = 256
HOPS = 2
KT = 2
LANES = 128
MC = 16
CORES = 2
MESH = pl.DeviceIdType.MESH


def kernel(
    states, members, slots,
    nbr_hbm, tix_hbm, cnt_hbm, cells_hbm, values_hbm, anom, tapers, out,
    nbr, tix, cnt, near_far, local, tab0, cells, values, obs_s, av, tv, r1, r2, tab_in, idx, innov, innov_in,
    hot, low, z, own_w, wr, v2, acc, part, got,
    tab_s, tab_r, idx_s, av_s, tv_s, s1, q1, s2, q2, s3, q3, relay_s, in_s, in_r, fs, fr, ps, pr, peers, entered,
):
    blocks, mem, width = anom.shape
    chunks = mem // MC
    last = chunks - 1
    groups = width // LANES
    cols = width // members
    none = KT * 3 * blocks
    d = lax.axis_index("state")
    me = lax.axis_index("member")
    odd = d % 2
    sign = 1 - 2 * odd
    heavy = chunks // 2
    fixed = 2 * HOPS + 1

    def at(ds, dm):
        return ((d + ds + states) % states, (me + dm) % members)

    barrier = pltpu.get_barrier_semaphore()
    greeted = [(sign, 0), (2 * sign, 0)]
    for ds, dm in greeted:
        pl.semaphore_signal(barrier, inc=1, device_id=at(ds, dm), device_id_type=MESH)

    @pl.when(d != states - 1)
    def _():
        for k in range(1, members):
            pl.semaphore_signal(barrier, inc=1, device_id=at(0, k), device_id_type=MESH)

    load_n = pltpu.make_async_copy(nbr_hbm, nbr, obs_s.at[2])
    load_x = pltpu.make_async_copy(tix_hbm, tix, obs_s.at[3])
    load_p = pltpu.make_async_copy(cnt_hbm, cnt, obs_s.at[4])
    load_a = pltpu.make_async_copy(anom, av, av_s)
    load_t = pltpu.make_async_copy(tapers, tv, tv_s)
    load_c = pltpu.make_async_copy(cells_hbm, cells, obs_s.at[0])
    load_v = pltpu.make_async_copy(values_hbm, values, obs_s.at[1])

    def remote(src, dst, send, recv, target):
        return pltpu.make_async_remote_copy(
            src_ref=src, dst_ref=dst, send_sem=send, recv_sem=recv,
            device_id=target, device_id_type=MESH,
        )

    def members_of(c, shift):
        return pl.ds(pl.multiple_of(((c + shift * heavy) % chunks) * MC, MC), MC)

    def columns_of(m):
        return pl.ds(pl.multiple_of(m * cols, cols), cols)

    def send2(c):
        return remote(
            anom.at[:, members_of(c, odd), :], r2.at[:, members_of(c, 0), :],
            s2.at[c], q2.at[c], at(-2 * sign, 0),
        )

    def send3(m):
        return remote(
            anom.at[:, members_of(last, odd), columns_of(m)],
            r2.at[:, members_of(last, 0), columns_of(m)],
            s3.at[m], q3.at[m], at(-2 * sign, 0),
        )

    def send1(c):
        return remote(
            anom.at[:, members_of(c, 1 - odd), :], r1.at[:, members_of(c, 0), :],
            s1.at[c], q1.at[c], at(sign, 0),
        )

    def relay():
        return remote(
            r1.at[:, members_of(heavy - 1, 0), columns_of(0)],
            r2.at[:, members_of(last, 0), columns_of(0)],
            relay_s, q3.at[0], at(-3, 0),
        )

    def to(u):
        return sign if u == 1 else -2 * sign

    def send_tab(u):
        return remote(near_far.at[u - 1], tab_in.at[u - 1], tab_s.at[u - 1], tab_r.at[u - 1], at(to(u), 0))

    def send_innov(u):
        where = columns_of(me) if u == 2 else pl.ds(0, width)
        return remote(
            innov.at[:, where], innov_in.at[u - 1, :, where], in_s.at[u - 1], in_r.at[u - 1], at(to(u), 0)
        )

    def share_innov(k, owner):
        where = columns_of(owner)
        return remote(
            innov_in.at[1, :, where], innov_in.at[1, :, where], fs.at[k], fr.at[k], at(0, k)
        )

    def send_part(u, m):
        return remote(
            part.at[u, m], got.at[u, me], ps.at[u, m], pr.at[u, me],
            ((d + (0, sign, 2 * sign)[u] + states) % states, m),
        )

    def part_from(u, m):
        return remote(part.at[u, m], got.at[u, m], ps.at[u, m], pr.at[u, m], at(sign, 0))

    pl.semaphore_wait(barrier, jnp.where(d == states - 1, len(greeted), len(greeted) + members - 1))
    send2(0).start()
    send1(0).start()
    for load in (load_n, load_x, load_p, load_c, load_v, load_a, load_t):
        load.start()
    acc[...] = jnp.zeros_like(acc)

    load_n.wait()
    load_x.wait()
    load_p.wait()
    row = lax.broadcasted_iota(jnp.int32, (blocks, slots), 0)
    slot = lax.broadcasted_iota(jnp.int32, (blocks, slots), 1)
    count = jnp.zeros((blocks, slots), jnp.int32)
    for i in range(blocks):
        count = jnp.where(row == i, cnt[i], count)
    valid = slot < count
    block = nbr[...]
    home = lax.div(block, jnp.int32(blocks))
    base = tix[...] * (3 * blocks) + block - home * blocks
    gap = home - d
    gap = jnp.where(gap > HOPS, gap - states, jnp.where(gap < -HOPS, gap + states, gap)) * sign
    near = jnp.where(gap == 1, base, jnp.where(gap == -1, base + 2 * blocks, none))
    far = jnp.where(gap == -2, base, jnp.where(gap == -1, base + blocks, none))
    near_far[...] = jnp.full(near_far.shape, none, jnp.int32)
    local[...] = jnp.full(local.shape, none, jnp.int32)
    near_far[0, :, 0:slots] = jnp.where(valid, near, none)
    near_far[1, :, 0:slots] = jnp.where(valid, far, none)
    local[0, :, 0:slots] = jnp.where(valid & (gap >= 0), base + gap * blocks, none)
    local[1, :, 0:slots] = jnp.where(valid & (gap == 0), base, none)
    local[2, :, 0:slots] = jnp.where(valid & (gap == 2), base + 2 * blocks, none)
    load_tab = pltpu.make_async_copy(local, tab0, obs_s.at[5])
    load_tab.start()
    for u in (1, 2):
        send_tab(u).start()

    @pl.when(d == states - 2)
    def _():
        for k in range(1, members):
            pl.semaphore_signal(entered, inc=1, device_id=at(0, k), device_id_type=MESH)
        pl.semaphore_wait(entered, members - 1)
        pl.semaphore_signal(entered, inc=1, device_id=at(sign, 0), device_id_type=MESH)

    def hot_row(k, carry):
        cell = cells[pl.ds(k, 1), :]
        value = values[pl.ds(k, 1), :]
        lo = cell & (LANES - 1)
        block = cell // width
        group = (cell // LANES) % groups
        hi = group * blocks + block
        v1 = value.astype(jnp.bfloat16).astype(jnp.float32)
        rest = value - v1
        v2 = rest.astype(jnp.bfloat16).astype(jnp.float32)
        v3 = rest - v2
        rows = blocks * groups
        same = lax.broadcasted_iota(jnp.int32, (rows, LANES), 0) == hi
        where = pl.ds(pl.multiple_of(k * LANES, LANES), LANES)
        for n, v in enumerate((v1, v2, v3)):
            hot[pl.ds(n * rows, rows), where] = jnp.where(
                same, jnp.broadcast_to(v, (rows, LANES)), 0.0
            ).astype(jnp.bfloat16)
        low[:, where] = jnp.where(
            lax.broadcasted_iota(jnp.int32, (LANES, LANES), 0) == lo, 1.0, 0.0
        ).astype(jnp.bfloat16)
        return carry

    load_c.wait()
    load_v.wait()
    lax.fori_loop(0, cells.shape[0], hot_row, 0)
    rows = blocks * groups
    sums = lax.dot_general(
        hot[...], low[...], (((1,), (1,)), ((), ())), preferred_element_type=jnp.float32
    )
    total = sums[0:rows] + sums[rows : 2 * rows] + sums[2 * rows : 3 * rows]
    for g in range(groups):
        innov[:, g * LANES : (g + 1) * LANES] = total[g * blocks : (g + 1) * blocks]
    for u in (1, 2):
        send_innov(u).start()
    for c in range(1, last):
        send2(c).start()

    @pl.when(d > 1)
    def _():
        send3(0).start()

    @pl.when(d != 1)
    def _():
        for m in range(1, members - 1):
            send3(m).start()

    @pl.when((d != 1) & (d != states - 2))
    def _():
        send3(members - 1).start()

    for c in range(1, heavy):
        send1(c).start()

    load_a.wait()
    for c in range(chunks):
        for j in range(blocks):
            own_w[c, j] = (
                av[j, members_of(c, odd), :].astype(jnp.float32) * innov[pl.ds(j, 1), :]
            ).astype(jnp.bfloat16)
    load_t.wait()

    def own_z(t, carry):
        res = lax.dot_general(
            own_w[...].reshape(chunks * blocks * MC, width), tv[t],
            (((1,), (1,)), ((), ())), preferred_element_type=jnp.float32,
        )
        z[:, pl.ds(t * 3 * blocks, blocks)] = res.reshape(chunks, blocks, MC, width)
        return carry

    lax.fori_loop(0, KT, own_z, 0)
    for c in range(heavy, chunks):
        for t in range(KT):
            z[c, (t * 3 + 1) * blocks : (t * 3 + 2) * blocks] = jnp.zeros((blocks, MC, width), jnp.float32)
    for c in range(chunks):
        z[c, none] = jnp.zeros((MC, width), jnp.float32)

    send_innov(2).wait_recv()

    @pl.when(d == states - 1)
    def _():
        pl.semaphore_wait(entered, 1)

    for k in range(1, members):
        share_innov(k, me).start()

    load_tab.wait()
    for u in (1, 2):
        send_tab(u).wait_recv()
        fill = pltpu.make_async_copy(tab_in.at[u - 1], idx.at[u - 1], idx_s.at[u - 1])
        fill.start()
        fill.wait()

    def offset_slot(g):
        return {-2: 1 + 3 * odd, -1: 2 + odd, 1: 3 - odd, 2: 4 - 3 * odd}[g]

    free = list(range(fixed, slots))

    def spread(c, table, i, named):
        total = z[c, table(i, named[0])]
        for s in named[1:] + free:
            total = total + z[c, table(i, s)]
        return total

    def pairs(c, u, table, named, source, shift):
        def one(i, carry):
            value = source[i, members_of(c, shift), :].astype(jnp.float32) * spread(c, table, i, named)
            acc[u, i] += jnp.sum(value.reshape(MC // 8, 8, width), axis=0)
            return carry

        lax.fori_loop(0, blocks, one, 0)

    def table0(k):
        return lambda i, s: tab0[k, i, s]

    def table_in(u):
        return lambda i, s: idx[u - 1, i, s]

    def fold(u):
        for i in range(blocks):
            line = jnp.sum(acc[u, i], axis=0, keepdims=True)
            for m in range(members):
                part[u, m, i : i + 1, :] = line[:, m * cols : (m + 1) * cols]

    def far_z(c, first):
        for g, r in enumerate((r1, r2)):
            if g or not first:
                for j in range(blocks):
                    wr[g * blocks + j] = (
                        r[j, members_of(c, 0), :].astype(jnp.float32)
                        * innov_in[g, pl.ds(j, 1), :]
                    ).astype(jnp.bfloat16)
        count = 2 * blocks - first

        def one(t, carry):
            res = lax.dot_general(
                wr[pl.ds(first, count)].reshape(count * MC, width), tv[t],
                (((1,), (1,)), ((), ())), preferred_element_type=jnp.float32,
            )
            z[c, pl.ds(t * 3 * blocks + blocks + first, count)] = res.reshape(count, MC, width)
            return carry

        lax.fori_loop(0, KT, one, 0)

    def full_step(c, carry):
        send2(c).wait_recv()
        send1(c).wait_recv()

        @pl.when((c == heavy - 1) & (d == 1))
        def _():
            relay().start()
            for m in range(members):
                send3(m).start()

        @pl.when(c == 0)
        def _():
            for k in range(1, members):
                pl.semaphore_signal(peers, inc=1, device_id=at(0, k), device_id_type=MESH)

        far_z(c, 0)
        pairs(c, 2, table_in(2), [offset_slot(-2), offset_slot(-1)], r2, 0)
        pairs(c, 1, table_in(1), [offset_slot(-1), offset_slot(1)], r1, 0)
        pairs(c, 0, table0(0), [0, offset_slot(1), offset_slot(2)], av, odd)
        return carry

    def ahead(c, carry):
        def one(i, carry):
            v2[c - heavy, i] = spread(c, table_in(2), i, [offset_slot(-2)])
            return carry

        lax.fori_loop(0, blocks, one, 0)
        pairs(c, 0, table0(1), [0], av, odd)
        return carry

    lax.fori_loop(heavy, chunks, ahead, 0)
    send_innov(1).wait_recv()
    for k in range(1, members):
        share_innov(k, (me + members - k) % members).wait_recv()
    lax.fori_loop(0, heavy, full_step, 0)
    fold(1)
    pl.semaphore_wait(peers, members - 1)
    for m in range(members):
        send_part(1, m).start()

    def reach(c):
        def one(i, carry):
            value = r2[i, members_of(c, 0), :].astype(jnp.float32) * v2[c - heavy, i]
            acc[2, i] += jnp.sum(value.reshape(MC // 8, 8, width), axis=0)
            return carry

        lax.fori_loop(0, blocks, one, 0)

    def fold_columns(u, m, i, value):
        where = columns_of(m)
        line = acc[u, i, :, where] + jnp.sum(value.reshape(MC // 8, 8, cols), axis=0)
        part[u, m, i : i + 1, :] = jnp.sum(line, axis=0, keepdims=True)

    def reach_columns(m):
        where = slice(m * cols, (m + 1) * cols)
        send3(m).wait_recv()
        for i in range(blocks):
            fold_columns(
                2, m, i,
                r2[i, members_of(last, 0), where].astype(jnp.float32) * v2[last - heavy, i, :, where],
            )
        send_part(2, m).start()

    def light_step(c, carry):
        send2(c).wait_recv()
        reach(c)

        @pl.when((d == states - 2) & (c == last - 1))
        def _():
            reach_columns(0)
            send3(members - 1).start()
            reach_columns(1)

        far_z(c, blocks)
        return carry

    lax.fori_loop(heavy, last, light_step, 0)

    def depth_z(m, t, where):
        inner = slice(m * cols, (m + 1) * cols)
        res = lax.dot_general(
            wr[blocks : 2 * blocks, :, inner].reshape(blocks * MC, cols), tv[t, where, inner],
            (((1,), (1,)), ((), ())), preferred_element_type=jnp.float32,
        ).reshape(blocks, MC, -1)
        panels = slice((t * 3 + 2) * blocks, (t * 3 + 3) * blocks)
        if m:
            res = z[last, panels, :, where] + res
        z[last, panels, :, where] = res

    for m in range(members):
        where = slice(m * cols, (m + 1) * cols)

        @pl.when(d != states - 2)
        def _():
            reach_columns(m)

        if m + 2 < members:
            @pl.when(d == states - 2)
            def _():
                reach_columns(m + 2)

        for j in range(blocks):
            wr[blocks + j, :, where] = (
                r2[j, members_of(last, 0), where].astype(jnp.float32) * innov_in[1, pl.ds(j, 1), where]
            ).astype(jnp.bfloat16)
        if m < members - 1:
            for t in range(KT):
                depth_z(m, t, pl.ds(0, width))
        if m == members - 2:
            for c in range(heavy, last):
                pairs(c, 0, table0(2), [offset_slot(2)], av, odd)

    chips = members // CORES
    order = [chip * CORES + core for chip in range(chips - 1, 0, -1) for core in range(CORES)]
    for away in order + list(range(CORES - 1, -1, -1)):
        m = (me // CORES + away // CORES) % chips * CORES + (me + away) % CORES
        where = columns_of(m)
        for t in range(KT):
            depth_z(members - 1, t, where)
        for i in range(blocks):
            total = z[last, tab0[2, i, offset_slot(2)], :, where]
            for s in free:
                total = total + z[last, tab0[2, i, s], :, where]
            fold_columns(0, m, i, av[i, members_of(last, odd), where].astype(jnp.float32) * total)
        if away:
            send_part(0, m).start()
    for u in (1, 2):
        send_tab(u).wait_send()
        send_innov(u).wait_send()
    for c in range(last):
        send2(c).wait_send()
    for m in range(1, members):
        send3(m).wait_send()

    @pl.when(d > 0)
    def _():
        send3(0).wait_send()

    @pl.when(d == 1)
    def _():
        relay().wait_send()

    for k in range(1, members):
        share_innov(k, me).wait_send()
    for c in range(heavy):
        send1(c).wait_send()
    for u in (1, 2):
        for m in range(members):
            send_part(u, m).wait_send()
    total = part[0, me]
    for u in (1, 2):
        for m in range(members):
            part_from(u, m).wait_recv()
            total = total + got[u, m]
    for k in range(1, members):
        m = (me + k) % members
        part_from(0, m).wait_recv()
        total = total + got[0, m]
    out[...] = total / jnp.float32(M - 1)
    for k in range(1, members):
        send_part(0, (me + k) % members).wait_send()


def on_device(states, members, anomalies, tapers, nbr_block, taper_index, pair_count, obs_cell, obs_value):
    blocks, mem, width = anomalies.shape
    slots = nbr_block.shape[1]
    chunks = mem // MC
    cols = width // members
    cells = obs_cell.reshape(-1, LANES)
    values = obs_value.reshape(-1, LANES)
    rows = blocks * (width // LANES)
    dma = pltpu.SemaphoreType.DMA
    any_space = pl.BlockSpec(memory_space=pl.ANY)
    vmem = pl.BlockSpec(memory_space=pltpu.VMEM)
    return pl.pallas_call(
        functools.partial(kernel, states, members, slots),
        out_shape=pltpu.VMEM((blocks, cols), jnp.float32),
        in_specs=[any_space] * 7,
        out_specs=vmem,
        scratch_shapes=[
            pltpu.VMEM(nbr_block.shape, jnp.int32),
            pltpu.VMEM(taper_index.shape, jnp.int32),
            pltpu.SMEM(pair_count.shape, jnp.int32),
            pltpu.VMEM((2, blocks, LANES), jnp.int32),
            pltpu.VMEM((3, blocks, LANES), jnp.int32),
            pltpu.SMEM((3, blocks, LANES), jnp.int32),
            pltpu.VMEM(cells.shape, jnp.int32),
            pltpu.VMEM(values.shape, jnp.float32),
            dma((6,)),
            pltpu.VMEM((blocks, mem, width), jnp.bfloat16),
            pltpu.VMEM(tapers.shape, jnp.bfloat16),
            pltpu.VMEM((blocks, mem, width), jnp.bfloat16),
            pltpu.VMEM((blocks, mem, width), jnp.bfloat16),
            pltpu.VMEM((2, blocks, LANES), jnp.int32),
            pltpu.SMEM((2, blocks, LANES), jnp.int32),
            pltpu.VMEM((blocks, width), jnp.float32),
            pltpu.VMEM((2, blocks, width), jnp.float32),
            pltpu.VMEM((3 * rows, obs_cell.shape[0]), jnp.bfloat16),
            pltpu.VMEM((LANES, obs_cell.shape[0]), jnp.bfloat16),
            pltpu.VMEM((chunks, KT * 3 * blocks + 1, MC, width), jnp.float32),
            pltpu.VMEM((chunks, blocks, MC, width), jnp.bfloat16),
            pltpu.VMEM((2 * blocks, MC, width), jnp.bfloat16),
            pltpu.VMEM((chunks // 2, blocks, MC, width), jnp.float32),
            pltpu.VMEM((3, blocks, 8, width), jnp.float32),
            pltpu.VMEM((3, members, blocks, cols), jnp.float32),
            pltpu.VMEM((3, members, blocks, cols), jnp.float32),
            dma((2,)), dma((2,)), dma((2,)), dma, dma,
            dma((chunks,)), dma((chunks,)),
            dma((chunks,)), dma((chunks,)),
            dma((members,)), dma((members,)), dma,
            dma((2,)), dma((2,)),
            dma((members,)), dma((members,)),
            dma((3, members)), dma((3, members)),
            pltpu.SemaphoreType.REGULAR,
            pltpu.SemaphoreType.REGULAR,
        ],
        compiler_params=pltpu.CompilerParams(
            collective_id=0, has_side_effects=True, vmem_limit_bytes=66_000_000
        ),
    )(nbr_block, taper_index, pair_count, cells, values, anomalies, tapers)


def solution(mesh):
    placed = (
        P("state", "member", None),
        P(),
        P("state", None),
        P("state", None),
        P("state"),
        P("state"),
        P("state"),
    )
    return jax.shard_map(
        functools.partial(on_device, mesh.shape["state"], mesh.shape["member"]),
        mesh=mesh, in_specs=placed, out_specs=P("state", "member"), check_vma=False,
    )
```

```python
import functools

import jax
import jax.numpy as jnp
from jax import lax
from jax.experimental import pallas as pl
from jax.experimental.pallas import tpu as pltpu
from jax.sharding import PartitionSpec as P

M = 256
HOPS = 2
KT = 2
LANES = 128
MC = 16
CORES = 2
MESH = pl.DeviceIdType.MESH


def kernel(
    states, members, slots,
    nbr_hbm, tix_hbm, cnt_hbm, cells_hbm, values_hbm, anom, tapers, out,
    nbr, tix, cnt, near_far, local, tab0, cells, values, obs_s, av, tv, r1, r2, tab_in, idx, innov, innov_in,
    hot, low, z, own_w, wr, v2, acc, part, got,
    tab_s, tab_r, idx_s, av_s, tv_s, s1, q1, s2, q2, s3, q3, relay_s, in_s, in_r, fs, fr, ps, pr, peers, entered,
):
    blocks, mem, width = anom.shape
    chunks = mem // MC
    last = chunks - 1
    groups = width // LANES
    cols = width // members
    none = KT * 3 * blocks
    d = lax.axis_index("state")
    me = lax.axis_index("member")
    odd = d % 2
    sign = 1 - 2 * odd
    heavy = chunks // 2
    fixed = 2 * HOPS + 1

    def at(ds, dm):
        return ((d + ds + states) % states, (me + dm) % members)

    barrier = pltpu.get_barrier_semaphore()
    greeted = [(sign, 0), (2 * sign, 0)]
    for ds, dm in greeted:
        pl.semaphore_signal(barrier, inc=1, device_id=at(ds, dm), device_id_type=MESH)

    @pl.when(d != states - 1)
    def _():
        for k in range(1, members):
            pl.semaphore_signal(barrier, inc=1, device_id=at(0, k), device_id_type=MESH)

    load_n = pltpu.make_async_copy(nbr_hbm, nbr, obs_s.at[2])
    load_x = pltpu.make_async_copy(tix_hbm, tix, obs_s.at[3])
    load_p = pltpu.make_async_copy(cnt_hbm, cnt, obs_s.at[4])
    load_a = pltpu.make_async_copy(anom, av, av_s)
    load_t = pltpu.make_async_copy(tapers, tv, tv_s)
    load_c = pltpu.make_async_copy(cells_hbm, cells, obs_s.at[0])
    load_v = pltpu.make_async_copy(values_hbm, values, obs_s.at[1])

    def remote(src, dst, send, recv, target):
        return pltpu.make_async_remote_copy(
            src_ref=src, dst_ref=dst, send_sem=send, recv_sem=recv,
            device_id=target, device_id_type=MESH,
        )

    def members_of(c, shift):
        return pl.ds(pl.multiple_of(((c + shift * heavy) % chunks) * MC, MC), MC)

    def columns_of(m):
        return pl.ds(pl.multiple_of(m * cols, cols), cols)

    def send2(c):
        return remote(
            anom.at[:, members_of(c, odd), :], r2.at[:, members_of(c, 0), :],
            s2.at[c], q2.at[c], at(-2 * sign, 0),
        )

    def send3(m):
        return remote(
            anom.at[:, members_of(last, odd), columns_of(m)],
            r2.at[:, members_of(last, 0), columns_of(m)],
            s3.at[m], q3.at[m], at(-2 * sign, 0),
        )

    def send1(c):
        return remote(
            anom.at[:, members_of(c, 1 - odd), :], r1.at[:, members_of(c, 0), :],
            s1.at[c], q1.at[c], at(sign, 0),
        )

    def relay():
        return remote(
            r1.at[:, members_of(heavy - 1, 0), columns_of(0)],
            r2.at[:, members_of(last, 0), columns_of(0)],
            relay_s, q3.at[0], at(-3, 0),
        )

    def to(u):
        return sign if u == 1 else -2 * sign

    def send_tab(u):
        return remote(near_far.at[u - 1], tab_in.at[u - 1], tab_s.at[u - 1], tab_r.at[u - 1], at(to(u), 0))

    def send_innov(u):
        where = columns_of(me) if u == 2 else pl.ds(0, width)
        return remote(
            innov.at[:, where], innov_in.at[u - 1, :, where], in_s.at[u - 1], in_r.at[u - 1], at(to(u), 0)
        )

    def share_innov(k, owner):
        where = columns_of(owner)
        return remote(
            innov_in.at[1, :, where], innov_in.at[1, :, where], fs.at[k], fr.at[k], at(0, k)
        )

    def send_part(u, m):
        return remote(
            part.at[u, m], got.at[u, me], ps.at[u, m], pr.at[u, me],
            ((d + (0, sign, 2 * sign)[u] + states) % states, m),
        )

    def part_from(u, m):
        return remote(part.at[u, m], got.at[u, m], ps.at[u, m], pr.at[u, m], at(sign, 0))

    pl.semaphore_wait(barrier, jnp.where(d == states - 1, len(greeted), len(greeted) + members - 1))
    send2(0).start()
    send1(0).start()
    for load in (load_n, load_x, load_p, load_c, load_v, load_a, load_t):
        load.start()
    acc[...] = jnp.zeros_like(acc)

    load_n.wait()
    load_x.wait()
    load_p.wait()
    row = lax.broadcasted_iota(jnp.int32, (blocks, slots), 0)
    slot = lax.broadcasted_iota(jnp.int32, (blocks, slots), 1)
    count = jnp.zeros((blocks, slots), jnp.int32)
    for i in range(blocks):
        count = jnp.where(row == i, cnt[i], count)
    valid = slot < count
    block = nbr[...]
    home = lax.div(block, jnp.int32(blocks))
    base = tix[...] * (3 * blocks) + block - home * blocks
    gap = home - d
    gap = jnp.where(gap > HOPS, gap - states, jnp.where(gap < -HOPS, gap + states, gap)) * sign
    near = jnp.where(gap == 1, base, jnp.where(gap == -1, base + 2 * blocks, none))
    far = jnp.where(gap == -2, base, jnp.where(gap == -1, base + blocks, none))
    near_far[...] = jnp.full(near_far.shape, none, jnp.int32)
    local[...] = jnp.full(local.shape, none, jnp.int32)
    near_far[0, :, 0:slots] = jnp.where(valid, near, none)
    near_far[1, :, 0:slots] = jnp.where(valid, far, none)
    local[0, :, 0:slots] = jnp.where(valid & (gap >= 0), base + gap * blocks, none)
    local[1, :, 0:slots] = jnp.where(valid & (gap == 0), base, none)
    local[2, :, 0:slots] = jnp.where(valid & (gap == 2), base + 2 * blocks, none)
    load_tab = pltpu.make_async_copy(local, tab0, obs_s.at[5])
    load_tab.start()
    for u in (1, 2):
        send_tab(u).start()

    @pl.when(d == states - 2)
    def _():
        for k in range(1, members):
            pl.semaphore_signal(entered, inc=1, device_id=at(0, k), device_id_type=MESH)
        pl.semaphore_wait(entered, members - 1)
        pl.semaphore_signal(entered, inc=1, device_id=at(sign, 0), device_id_type=MESH)

    def hot_row(k, carry):
        cell = cells[pl.ds(k, 1), :]
        value = values[pl.ds(k, 1), :]
        lo = cell & (LANES - 1)
        block = cell // width
        group = (cell // LANES) % groups
        hi = group * blocks + block
        v1 = value.astype(jnp.bfloat16).astype(jnp.float32)
        rest = value - v1
        v2 = rest.astype(jnp.bfloat16).astype(jnp.float32)
        v3 = rest - v2
        rows = blocks * groups
        same = lax.broadcasted_iota(jnp.int32, (rows, LANES), 0) == hi
        where = pl.ds(pl.multiple_of(k * LANES, LANES), LANES)
        for n, v in enumerate((v1, v2, v3)):
            hot[pl.ds(n * rows, rows), where] = jnp.where(
                same, jnp.broadcast_to(v, (rows, LANES)), 0.0
            ).astype(jnp.bfloat16)
        low[:, where] = jnp.where(
            lax.broadcasted_iota(jnp.int32, (LANES, LANES), 0) == lo, 1.0, 0.0
        ).astype(jnp.bfloat16)
        return carry

    load_c.wait()
    load_v.wait()
    lax.fori_loop(0, cells.shape[0], hot_row, 0)
    rows = blocks * groups
    sums = lax.dot_general(
        hot[...], low[...], (((1,), (1,)), ((), ())), preferred_element_type=jnp.float32
    )
    total = sums[0:rows] + sums[rows : 2 * rows] + sums[2 * rows : 3 * rows]
    for g in range(groups):
        innov[:, g * LANES : (g + 1) * LANES] = total[g * blocks : (g + 1) * blocks]
    for u in (1, 2):
        send_innov(u).start()
    for c in range(1, last):
        send2(c).start()

    @pl.when(d > 1)
    def _():
        send3(0).start()

    @pl.when(d != 1)
    def _():
        for m in range(1, members - 1):
            send3(m).start()

    @pl.when((d != 1) & (d != states - 2))
    def _():
        send3(members - 1).start()

    for c in range(1, heavy):
        send1(c).start()

    load_a.wait()
    for c in range(chunks):
        for j in range(blocks):
            own_w[c, j] = (
                av[j, members_of(c, odd), :].astype(jnp.float32) * innov[pl.ds(j, 1), :]
            ).astype(jnp.bfloat16)
    load_t.wait()

    def own_z(t, carry):
        res = lax.dot_general(
            own_w[...].reshape(chunks * blocks * MC, width), tv[t],
            (((1,), (1,)), ((), ())), preferred_element_type=jnp.float32,
        )
        z[:, pl.ds(t * 3 * blocks, blocks)] = res.reshape(chunks, blocks, MC, width)
        return carry

    lax.fori_loop(0, KT, own_z, 0)
    for c in range(heavy, chunks):
        for t in range(KT):
            z[c, (t * 3 + 1) * blocks : (t * 3 + 2) * blocks] = jnp.zeros((blocks, MC, width), jnp.float32)
    for c in range(chunks):
        z[c, none] = jnp.zeros((MC, width), jnp.float32)

    send_innov(2).wait_recv()

    @pl.when(d == states - 1)
    def _():
        pl.semaphore_wait(entered, 1)

    for k in range(1, members):
        share_innov(k, me).start()

    load_tab.wait()
    for u in (1, 2):
        send_tab(u).wait_recv()
        fill = pltpu.make_async_copy(tab_in.at[u - 1], idx.at[u - 1], idx_s.at[u - 1])
        fill.start()
        fill.wait()

    def offset_slot(g):
        return {-2: 1 + 3 * odd, -1: 2 + odd, 1: 3 - odd, 2: 4 - 3 * odd}[g]

    free = list(range(fixed, slots))

    def spread(c, table, i, named):
        total = z[c, table(i, named[0])]
        for s in named[1:] + free:
            total = total + z[c, table(i, s)]
        return total

    def pairs(c, u, table, named, source, shift):
        def one(i, carry):
            value = source[i, members_of(c, shift), :].astype(jnp.float32) * spread(c, table, i, named)
            acc[u, i] += jnp.sum(value.reshape(MC // 8, 8, width), axis=0)
            return carry

        lax.fori_loop(0, blocks, one, 0)

    def table0(k):
        return lambda i, s: tab0[k, i, s]

    def table_in(u):
        return lambda i, s: idx[u - 1, i, s]

    def fold(u):
        for i in range(blocks):
            line = jnp.sum(acc[u, i], axis=0, keepdims=True)
            for m in range(members):
                part[u, m, i : i + 1, :] = line[:, m * cols : (m + 1) * cols]

    def far_z(c, first):
        for g, r in enumerate((r1, r2)):
            if g or not first:
                for j in range(blocks):
                    wr[g * blocks + j] = (
                        r[j, members_of(c, 0), :].astype(jnp.float32)
                        * innov_in[g, pl.ds(j, 1), :]
                    ).astype(jnp.bfloat16)
        count = 2 * blocks - first

        def one(t, carry):
            res = lax.dot_general(
                wr[pl.ds(first, count)].reshape(count * MC, width), tv[t],
                (((1,), (1,)), ((), ())), preferred_element_type=jnp.float32,
            )
            z[c, pl.ds(t * 3 * blocks + blocks + first, count)] = res.reshape(count, MC, width)
            return carry

        lax.fori_loop(0, KT, one, 0)

    def full_step(c, carry):
        send2(c).wait_recv()
        send1(c).wait_recv()

        @pl.when((c == heavy - 1) & (d == 1))
        def _():
            relay().start()
            for m in range(members):
                send3(m).start()

        @pl.when(c == 0)
        def _():
            for k in range(1, members):
                pl.semaphore_signal(peers, inc=1, device_id=at(0, k), device_id_type=MESH)

        far_z(c, 0)
        pairs(c, 2, table_in(2), [offset_slot(-2), offset_slot(-1)], r2, 0)
        pairs(c, 1, table_in(1), [offset_slot(-1), offset_slot(1)], r1, 0)
        pairs(c, 0, table0(0), [0, offset_slot(1), offset_slot(2)], av, odd)
        return carry

    def ahead(c, carry):
        def one(i, carry):
            v2[c - heavy, i] = spread(c, table_in(2), i, [offset_slot(-2)])
            return carry

        lax.fori_loop(0, blocks, one, 0)
        pairs(c, 0, table0(1), [0], av, odd)
        return carry

    lax.fori_loop(heavy, chunks, ahead, 0)
    send_innov(1).wait_recv()
    for k in range(1, members):
        share_innov(k, (me + members - k) % members).wait_recv()
    lax.fori_loop(0, heavy, full_step, 0)
    fold(1)
    pl.semaphore_wait(peers, members - 1)
    for m in range(members):
        send_part(1, m).start()

    def reach(c):
        def one(i, carry):
            value = r2[i, members_of(c, 0), :].astype(jnp.float32) * v2[c - heavy, i]
            acc[2, i] += jnp.sum(value.reshape(MC // 8, 8, width), axis=0)
            return carry

        lax.fori_loop(0, blocks, one, 0)

    def fold_columns(u, m, values):
        where = columns_of(m)
        lines = [jnp.sum(value.reshape(MC // 8, 8, cols), axis=0) for value in values]
        part[u, m] = jnp.sum(acc[u, :, :, where] + jnp.stack(lines), axis=1)

    def reach_columns(m):
        where = slice(m * cols, (m + 1) * cols)
        send3(m).wait_recv()
        fold_columns(2, m, [
            r2[i, members_of(last, 0), where].astype(jnp.float32) * v2[last - heavy, i, :, where]
            for i in range(blocks)
        ])
        send_part(2, m).start()

    def light_step(c, carry):
        send2(c).wait_recv()
        reach(c)

        @pl.when((d == states - 2) & (c == last - 1))
        def _():
            reach_columns(0)
            send3(members - 1).start()
            reach_columns(1)

        far_z(c, blocks)
        return carry

    lax.fori_loop(heavy, last, light_step, 0)

    def depth_z(m, t, where):
        inner = slice(m * cols, (m + 1) * cols)
        res = lax.dot_general(
            wr[blocks : 2 * blocks, :, inner].reshape(blocks * MC, cols), tv[t, where, inner],
            (((1,), (1,)), ((), ())), preferred_element_type=jnp.float32,
        ).reshape(blocks, MC, -1)
        panels = slice((t * 3 + 2) * blocks, (t * 3 + 3) * blocks)
        if m:
            res = z[last, panels, :, where] + res
        z[last, panels, :, where] = res

    for m in range(members):
        where = slice(m * cols, (m + 1) * cols)

        @pl.when(d != states - 2)
        def _():
            reach_columns(m)

        if m + 2 < members:
            @pl.when(d == states - 2)
            def _():
                reach_columns(m + 2)

        for j in range(blocks):
            wr[blocks + j, :, where] = (
                r2[j, members_of(last, 0), where].astype(jnp.float32) * innov_in[1, pl.ds(j, 1), where]
            ).astype(jnp.bfloat16)
        if m < members - 1:
            for t in range(KT):
                depth_z(m, t, pl.ds(0, width))
        if m == members - 2:
            for c in range(heavy, last):
                pairs(c, 0, table0(2), [offset_slot(2)], av, odd)

    chips = members // CORES
    order = [chip * CORES + core for chip in range(chips - 1, 0, -1) for core in range(CORES)]
    for away in order + list(range(CORES - 1, -1, -1)):
        m = (me // CORES + away // CORES) % chips * CORES + (me + away) % CORES
        where = columns_of(m)
        for t in range(KT):
            depth_z(members - 1, t, where)
        values = []
        for i in range(blocks):
            total = z[last, tab0[2, i, offset_slot(2)], :, where]
            for s in free:
                total = total + z[last, tab0[2, i, s], :, where]
            values.append(av[i, members_of(last, odd), where].astype(jnp.float32) * total)
        fold_columns(0, m, values)
        if away:
            send_part(0, m).start()
    for u in (1, 2):
        send_tab(u).wait_send()
        send_innov(u).wait_send()
    for c in range(last):
        send2(c).wait_send()
    for m in range(1, members):
        send3(m).wait_send()

    @pl.when(d > 0)
    def _():
        send3(0).wait_send()

    @pl.when(d == 1)
    def _():
        relay().wait_send()

    for k in range(1, members):
        share_innov(k, me).wait_send()
    for c in range(heavy):
        send1(c).wait_send()
    for u in (1, 2):
        for m in range(members):
            send_part(u, m).wait_send()
    total = part[0, me]
    for u in (1, 2):
        for m in range(members):
            part_from(u, m).wait_recv()
            total = total + got[u, m]
    for k in range(1, members):
        m = (me + k) % members
        part_from(0, m).wait_recv()
        total = total + got[0, m]
    out[...] = total / jnp.float32(M - 1)
    for k in range(1, members):
        send_part(0, (me + k) % members).wait_send()


def on_device(states, members, anomalies, tapers, nbr_block, taper_index, pair_count, obs_cell, obs_value):
    blocks, mem, width = anomalies.shape
    slots = nbr_block.shape[1]
    chunks = mem // MC
    cols = width // members
    cells = obs_cell.reshape(-1, LANES)
    values = obs_value.reshape(-1, LANES)
    rows = blocks * (width // LANES)
    dma = pltpu.SemaphoreType.DMA
    any_space = pl.BlockSpec(memory_space=pl.ANY)
    vmem = pl.BlockSpec(memory_space=pltpu.VMEM)
    return pl.pallas_call(
        functools.partial(kernel, states, members, slots),
        out_shape=pltpu.VMEM((blocks, cols), jnp.float32),
        in_specs=[any_space] * 7,
        out_specs=vmem,
        scratch_shapes=[
            pltpu.VMEM(nbr_block.shape, jnp.int32),
            pltpu.VMEM(taper_index.shape, jnp.int32),
            pltpu.SMEM(pair_count.shape, jnp.int32),
            pltpu.VMEM((2, blocks, LANES), jnp.int32),
            pltpu.VMEM((3, blocks, LANES), jnp.int32),
            pltpu.SMEM((3, blocks, LANES), jnp.int32),
            pltpu.VMEM(cells.shape, jnp.int32),
            pltpu.VMEM(values.shape, jnp.float32),
            dma((6,)),
            pltpu.VMEM((blocks, mem, width), jnp.bfloat16),
            pltpu.VMEM(tapers.shape, jnp.bfloat16),
            pltpu.VMEM((blocks, mem, width), jnp.bfloat16),
            pltpu.VMEM((blocks, mem, width), jnp.bfloat16),
            pltpu.VMEM((2, blocks, LANES), jnp.int32),
            pltpu.SMEM((2, blocks, LANES), jnp.int32),
            pltpu.VMEM((blocks, width), jnp.float32),
            pltpu.VMEM((2, blocks, width), jnp.float32),
            pltpu.VMEM((3 * rows, obs_cell.shape[0]), jnp.bfloat16),
            pltpu.VMEM((LANES, obs_cell.shape[0]), jnp.bfloat16),
            pltpu.VMEM((chunks, KT * 3 * blocks + 1, MC, width), jnp.float32),
            pltpu.VMEM((chunks, blocks, MC, width), jnp.bfloat16),
            pltpu.VMEM((2 * blocks, MC, width), jnp.bfloat16),
            pltpu.VMEM((chunks // 2, blocks, MC, width), jnp.float32),
            pltpu.VMEM((3, blocks, 8, width), jnp.float32),
            pltpu.VMEM((3, members, blocks, cols), jnp.float32),
            pltpu.VMEM((3, members, blocks, cols), jnp.float32),
            dma((2,)), dma((2,)), dma((2,)), dma, dma,
            dma((chunks,)), dma((chunks,)),
            dma((chunks,)), dma((chunks,)),
            dma((members,)), dma((members,)), dma,
            dma((2,)), dma((2,)),
            dma((members,)), dma((members,)),
            dma((3, members)), dma((3, members)),
            pltpu.SemaphoreType.REGULAR,
            pltpu.SemaphoreType.REGULAR,
        ],
        compiler_params=pltpu.CompilerParams(
            collective_id=0, has_side_effects=True, vmem_limit_bytes=66_000_000
        ),
    )(nbr_block, taper_index, pair_count, cells, values, anomalies, tapers)


def solution(mesh):
    placed = (
        P("state", "member", None),
        P(),
        P("state", None),
        P("state", None),
        P("state"),
        P("state"),
        P("state"),
    )
    return jax.shard_map(
        functools.partial(on_device, mesh.shape["state"], mesh.shape["member"]),
        mesh=mesh, in_specs=placed, out_specs=P("state", "member"), check_vma=False,
    )
```

```python
import functools

import jax
import jax.numpy as jnp
from jax import lax
from jax.experimental import pallas as pl
from jax.experimental.pallas import tpu as pltpu
from jax.sharding import PartitionSpec as P

M = 256
HOPS = 2
KT = 2
LANES = 128
MC = 16
CORES = 2
MESH = pl.DeviceIdType.MESH


def kernel(
    states, members, slots,
    nbr_hbm, tix_hbm, cnt_hbm, cells_hbm, values_hbm, anom, tapers, out,
    nbr, tix, cnt, near_far, local, tab0, cells, values, obs_s, av, tv, r1, r2, tab_in, idx, innov, innov_in,
    hot, low, z, own_w, wr, v2, acc, part, got,
    tab_s, tab_r, idx_s, av_s, tv_s, s1, q1, s2, q2, s3, q3, relay_s, in_s, in_r, fs, fr, ps, pr, peers, entered,
):
    blocks, mem, width = anom.shape
    chunks = mem // MC
    last = chunks - 1
    groups = width // LANES
    cols = width // members
    none = KT * 3 * blocks
    d = lax.axis_index("state")
    me = lax.axis_index("member")
    odd = d % 2
    sign = 1 - 2 * odd
    heavy = chunks // 2
    fixed = 2 * HOPS + 1

    def at(ds, dm):
        return ((d + ds + states) % states, (me + dm) % members)

    barrier = pltpu.get_barrier_semaphore()
    greeted = [(sign, 0), (2 * sign, 0)]
    for ds, dm in greeted:
        pl.semaphore_signal(barrier, inc=1, device_id=at(ds, dm), device_id_type=MESH)

    @pl.when(d != states - 1)
    def _():
        for k in range(1, members):
            pl.semaphore_signal(barrier, inc=1, device_id=at(0, k), device_id_type=MESH)

    load_n = pltpu.make_async_copy(nbr_hbm, nbr, obs_s.at[2])
    load_x = pltpu.make_async_copy(tix_hbm, tix, obs_s.at[3])
    load_p = pltpu.make_async_copy(cnt_hbm, cnt, obs_s.at[4])
    load_a = pltpu.make_async_copy(anom, av, av_s)
    load_t = pltpu.make_async_copy(tapers, tv, tv_s)
    load_c = pltpu.make_async_copy(cells_hbm, cells, obs_s.at[0])
    load_v = pltpu.make_async_copy(values_hbm, values, obs_s.at[1])

    def remote(src, dst, send, recv, target):
        return pltpu.make_async_remote_copy(
            src_ref=src, dst_ref=dst, send_sem=send, recv_sem=recv,
            device_id=target, device_id_type=MESH,
        )

    def members_of(c, shift):
        return pl.ds(pl.multiple_of(((c + shift * heavy) % chunks) * MC, MC), MC)

    def columns_of(m):
        return pl.ds(pl.multiple_of(m * cols, cols), cols)

    def send2(c):
        return remote(
            anom.at[:, members_of(c, odd), :], r2.at[:, members_of(c, 0), :],
            s2.at[c], q2.at[c], at(-2 * sign, 0),
        )

    def send3(m):
        return remote(
            anom.at[:, members_of(last, odd), columns_of(m)],
            r2.at[:, members_of(last, 0), columns_of(m)],
            s3.at[m], q3.at[m], at(-2 * sign, 0),
        )

    def send1(c):
        return remote(
            anom.at[:, members_of(c, 1 - odd), :], r1.at[:, members_of(c, 0), :],
            s1.at[c], q1.at[c], at(sign, 0),
        )

    def relay():
        return remote(
            r1.at[:, members_of(heavy - 1, 0), columns_of(0)],
            r2.at[:, members_of(last, 0), columns_of(0)],
            relay_s, q3.at[0], at(-3, 0),
        )

    def to(u):
        return sign if u == 1 else -2 * sign

    def send_tab(u):
        return remote(near_far.at[u - 1], tab_in.at[u - 1], tab_s.at[u - 1], tab_r.at[u - 1], at(to(u), 0))

    def send_innov(u):
        where = columns_of(me) if u == 2 else pl.ds(0, width)
        return remote(
            innov.at[:, where], innov_in.at[u - 1, :, where], in_s.at[u - 1], in_r.at[u - 1], at(to(u), 0)
        )

    def share_innov(k, owner):
        where = columns_of(owner)
        return remote(
            innov_in.at[1, :, where], innov_in.at[1, :, where], fs.at[k], fr.at[k], at(0, k)
        )

    def send_part(u, m):
        return remote(
            part.at[u, m], got.at[u, me], ps.at[u, m], pr.at[u, me],
            ((d + (0, sign, 2 * sign)[u] + states) % states, m),
        )

    def part_from(u, m):
        return remote(part.at[u, m], got.at[u, m], ps.at[u, m], pr.at[u, m], at(sign, 0))

    pl.semaphore_wait(barrier, jnp.where(d == states - 1, len(greeted), len(greeted) + members - 1))
    send2(0).start()
    send1(0).start()
    for load in (load_n, load_x, load_p, load_c, load_v, load_a, load_t):
        load.start()
    acc[...] = jnp.zeros_like(acc)

    load_n.wait()
    load_x.wait()
    load_p.wait()
    row = lax.broadcasted_iota(jnp.int32, (blocks, slots), 0)
    slot = lax.broadcasted_iota(jnp.int32, (blocks, slots), 1)
    count = jnp.zeros((blocks, slots), jnp.int32)
    for i in range(blocks):
        count = jnp.where(row == i, cnt[i], count)
    valid = slot < count
    block = nbr[...]
    home = lax.div(block, jnp.int32(blocks))
    base = tix[...] * (3 * blocks) + block - home * blocks
    gap = home - d
    gap = jnp.where(gap > HOPS, gap - states, jnp.where(gap < -HOPS, gap + states, gap)) * sign
    near = jnp.where(gap == 1, base, jnp.where(gap == -1, base + 2 * blocks, none))
    far = jnp.where(gap == -2, base, jnp.where(gap == -1, base + blocks, none))
    near_far[...] = jnp.full(near_far.shape, none, jnp.int32)
    local[...] = jnp.full(local.shape, none, jnp.int32)
    near_far[0, :, 0:slots] = jnp.where(valid, near, none)
    near_far[1, :, 0:slots] = jnp.where(valid, far, none)
    local[0, :, 0:slots] = jnp.where(valid & (gap >= 0), base + gap * blocks, none)
    local[1, :, 0:slots] = jnp.where(valid & (gap == 0), base, none)
    local[2, :, 0:slots] = jnp.where(valid & (gap == 2), base + 2 * blocks, none)
    load_tab = pltpu.make_async_copy(local, tab0, obs_s.at[5])
    load_tab.start()
    for u in (1, 2):
        send_tab(u).start()

    @pl.when(d == states - 2)
    def _():
        for k in range(1, members):
            pl.semaphore_signal(entered, inc=1, device_id=at(0, k), device_id_type=MESH)
        pl.semaphore_wait(entered, members - 1)
        pl.semaphore_signal(entered, inc=1, device_id=at(sign, 0), device_id_type=MESH)

    def hot_row(k, carry):
        cell = cells[pl.ds(k, 1), :]
        value = values[pl.ds(k, 1), :]
        lo = cell & (LANES - 1)
        block = cell // width
        group = (cell // LANES) % groups
        hi = group * blocks + block
        v1 = value.astype(jnp.bfloat16).astype(jnp.float32)
        rest = value - v1
        v2 = rest.astype(jnp.bfloat16).astype(jnp.float32)
        v3 = rest - v2
        rows = blocks * groups
        same = lax.broadcasted_iota(jnp.int32, (rows, LANES), 0) == hi
        where = pl.ds(pl.multiple_of(k * LANES, LANES), LANES)
        for n, v in enumerate((v1, v2, v3)):
            hot[pl.ds(n * rows, rows), where] = jnp.where(
                same, jnp.broadcast_to(v, (rows, LANES)), 0.0
            ).astype(jnp.bfloat16)
        low[:, where] = jnp.where(
            lax.broadcasted_iota(jnp.int32, (LANES, LANES), 0) == lo, 1.0, 0.0
        ).astype(jnp.bfloat16)
        return carry

    load_c.wait()
    load_v.wait()
    lax.fori_loop(0, cells.shape[0], hot_row, 0)
    rows = blocks * groups
    sums = lax.dot_general(
        hot[...], low[...], (((1,), (1,)), ((), ())), preferred_element_type=jnp.float32
    )
    total = sums[0:rows] + sums[rows : 2 * rows] + sums[2 * rows : 3 * rows]
    for g in range(groups):
        innov[:, g * LANES : (g + 1) * LANES] = total[g * blocks : (g + 1) * blocks]
    for u in (1, 2):
        send_innov(u).start()
    for c in range(1, last):
        send2(c).start()

    @pl.when(d > 1)
    def _():
        send3(0).start()

    @pl.when(d != 1)
    def _():
        for m in range(1, members - 1):
            send3(m).start()

    @pl.when((d != 1) & (d != states - 2))
    def _():
        send3(members - 1).start()

    for c in range(1, heavy):
        send1(c).start()

    load_a.wait()
    for c in range(chunks):
        for j in range(blocks):
            own_w[c, j] = (
                av[j, members_of(c, odd), :].astype(jnp.float32) * innov[pl.ds(j, 1), :]
            ).astype(jnp.bfloat16)
    load_t.wait()

    def own_z(t, carry):
        res = lax.dot_general(
            own_w[...].reshape(chunks * blocks * MC, width), tv[t],
            (((1,), (1,)), ((), ())), preferred_element_type=jnp.float32,
        )
        z[:, pl.ds(t * 3 * blocks, blocks)] = res.reshape(chunks, blocks, MC, width)
        return carry

    lax.fori_loop(0, KT, own_z, 0)
    for c in range(heavy, chunks):
        for t in range(KT):
            z[c, (t * 3 + 1) * blocks : (t * 3 + 2) * blocks] = jnp.zeros((blocks, MC, width), jnp.float32)
    for c in range(chunks):
        z[c, none] = jnp.zeros((MC, width), jnp.float32)

    send_innov(2).wait_recv()

    @pl.when(d == states - 1)
    def _():
        pl.semaphore_wait(entered, 1)

    for k in range(1, members):
        share_innov(k, me).start()

    load_tab.wait()
    for u in (1, 2):
        send_tab(u).wait_recv()
        fill = pltpu.make_async_copy(tab_in.at[u - 1], idx.at[u - 1], idx_s.at[u - 1])
        fill.start()
        fill.wait()

    def offset_slot(g):
        return {-2: 1 + 3 * odd, -1: 2 + odd, 1: 3 - odd, 2: 4 - 3 * odd}[g]

    free = list(range(fixed, slots))

    def spread(c, table, i, named):
        total = z[c, table(i, named[0])]
        for s in named[1:] + free:
            total = total + z[c, table(i, s)]
        return total

    def pairs(c, u, table, named, source, shift):
        def one(i, carry):
            value = source[i, members_of(c, shift), :].astype(jnp.float32) * spread(c, table, i, named)
            acc[u, i] += jnp.sum(value.reshape(MC // 8, 8, width), axis=0)
            return carry

        lax.fori_loop(0, blocks, one, 0)

    def table0(k):
        return lambda i, s: tab0[k, i, s]

    def table_in(u):
        return lambda i, s: idx[u - 1, i, s]

    def fold(u):
        for i in range(blocks):
            line = jnp.sum(acc[u, i], axis=0, keepdims=True)
            for m in range(members):
                part[u, m, i : i + 1, :] = line[:, m * cols : (m + 1) * cols]

    def far_z(c, first):
        for g, r in enumerate((r1, r2)):
            if g or not first:
                for j in range(blocks):
                    wr[g * blocks + j] = (
                        r[j, members_of(c, 0), :].astype(jnp.float32)
                        * innov_in[g, pl.ds(j, 1), :]
                    ).astype(jnp.bfloat16)
        count = 2 * blocks - first

        def one(t, carry):
            res = lax.dot_general(
                wr[pl.ds(first, count)].reshape(count * MC, width), tv[t],
                (((1,), (1,)), ((), ())), preferred_element_type=jnp.float32,
            )
            z[c, pl.ds(t * 3 * blocks + blocks + first, count)] = res.reshape(count, MC, width)
            return carry

        lax.fori_loop(0, KT, one, 0)

    def full_step(c, carry):
        send2(c).wait_recv()
        send1(c).wait_recv()

        @pl.when((c == heavy - 1) & (d == 1))
        def _():
            relay().start()
            for m in range(members):
                send3(m).start()

        @pl.when(c == 0)
        def _():
            for k in range(1, members):
                pl.semaphore_signal(peers, inc=1, device_id=at(0, k), device_id_type=MESH)

        far_z(c, 0)
        pairs(c, 2, table_in(2), [offset_slot(-2), offset_slot(-1)], r2, 0)
        pairs(c, 1, table_in(1), [offset_slot(-1), offset_slot(1)], r1, 0)
        pairs(c, 0, table0(0), [0, offset_slot(1), offset_slot(2)], av, odd)
        return carry

    def ahead(c, carry):
        def one(i, carry):
            v2[c - heavy, i] = spread(c, table_in(2), i, [offset_slot(-2)])
            return carry

        lax.fori_loop(0, blocks, one, 0)
        pairs(c, 0, table0(1), [0], av, odd)
        return carry

    lax.fori_loop(heavy, chunks, ahead, 0)
    send_innov(1).wait_recv()
    for k in range(1, members):
        share_innov(k, (me + members - k) % members).wait_recv()
    lax.fori_loop(0, heavy, full_step, 0)
    fold(1)
    pl.semaphore_wait(peers, members - 1)
    for m in range(members):
        send_part(1, m).start()

    def reach(c):
        def one(i, carry):
            value = r2[i, members_of(c, 0), :].astype(jnp.float32) * v2[c - heavy, i]
            acc[2, i] += jnp.sum(value.reshape(MC // 8, 8, width), axis=0)
            return carry

        lax.fori_loop(0, blocks, one, 0)

    def fold_columns(u, m, values):
        where = columns_of(m)
        lines = [jnp.sum(value.reshape(MC // 8, 8, cols), axis=0) for value in values]
        part[u, m] = jnp.sum(acc[u, :, :, where] + jnp.stack(lines), axis=1)

    def reach_columns(m):
        where = slice(m * cols, (m + 1) * cols)
        send3(m).wait_recv()
        fold_columns(2, m, [
            r2[i, members_of(last, 0), where].astype(jnp.float32) * v2[last - heavy, i, :, where]
            for i in range(blocks)
        ])
        send_part(2, m).start()

    def light_step(c, carry):
        send2(c).wait_recv()
        reach(c)

        @pl.when((d == states - 2) & (c == last - 1))
        def _():
            reach_columns(0)
            send3(members - 1).start()
            reach_columns(1)

        far_z(c, blocks)
        return carry

    lax.fori_loop(heavy, last, light_step, 0)

    def depth_z(m, t, where):
        inner = slice(m * cols, (m + 1) * cols)
        res = lax.dot_general(
            wr[blocks : 2 * blocks, :, inner].reshape(blocks * MC, cols), tv[t, where, inner],
            (((1,), (1,)), ((), ())), preferred_element_type=jnp.float32,
        ).reshape(blocks, MC, -1)
        panels = slice((t * 3 + 2) * blocks, (t * 3 + 3) * blocks)
        if m:
            res = z[last, panels, :, where] + res
        z[last, panels, :, where] = res

    for m in range(members):
        where = slice(m * cols, (m + 1) * cols)

        @pl.when(d != states - 2)
        def _():
            reach_columns(m)

        if m + 2 < members:
            @pl.when(d == states - 2)
            def _():
                reach_columns(m + 2)

        for j in range(blocks):
            wr[blocks + j, :, where] = (
                r2[j, members_of(last, 0), where].astype(jnp.float32) * innov_in[1, pl.ds(j, 1), where]
            ).astype(jnp.bfloat16)
        if m < members - 1:
            for t in range(KT):
                depth_z(m, t, pl.ds(0, width))
        if m == members - 2:
            for c in range(heavy, last):
                pairs(c, 0, table0(2), [offset_slot(2)], av, odd)

    chips = members // CORES
    order = [chip * CORES + core for chip in range(chips - 1, 0, -1) for core in range(CORES)]
    for away in order + list(range(CORES - 1, -1, -1)):
        m = (me // CORES + away // CORES) % chips * CORES + (me + away) % CORES
        where = columns_of(m)
        for t in range(KT):
            depth_z(members - 1, t, where)
        values = []
        for i in range(blocks):
            total = z[last, tab0[2, i, offset_slot(2)], :, where]
            for s in free:
                total = total + z[last, tab0[2, i, s], :, where]
            values.append(av[i, members_of(last, odd), where].astype(jnp.float32) * total)
        fold_columns(0, m, values)
        if away:
            send_part(0, m).start()
    for u in (1, 2):
        send_tab(u).wait_send()
        send_innov(u).wait_send()
    for c in range(last):
        send2(c).wait_send()
    for m in range(1, members):
        send3(m).wait_send()

    @pl.when(d > 0)
    def _():
        send3(0).wait_send()

    @pl.when(d == 1)
    def _():
        relay().wait_send()

    for k in range(1, members):
        share_innov(k, me).wait_send()
    for c in range(heavy):
        send1(c).wait_send()
    for u in (1, 2):
        for m in range(members):
            send_part(u, m).wait_send()
    total = part[0, me]
    for u in (1, 2):
        for m in range(members):
            part_from(u, m).wait_recv()
            total = total + got[u, m]
    for k in range(1, members):
        m = (me + k) % members
        part_from(0, m).wait_recv()
        total = total + got[0, m]
    out[...] = total
    for k in range(1, members):
        send_part(0, (me + k) % members).wait_send()


def on_device(states, members, anomalies, tapers, nbr_block, taper_index, pair_count, obs_cell, obs_value):
    blocks, mem, width = anomalies.shape
    slots = nbr_block.shape[1]
    chunks = mem // MC
    cols = width // members
    cells = obs_cell.reshape(-1, LANES)
    values = obs_value.reshape(-1, LANES)
    rows = blocks * (width // LANES)
    dma = pltpu.SemaphoreType.DMA
    any_space = pl.BlockSpec(memory_space=pl.ANY)
    vmem = pl.BlockSpec(memory_space=pltpu.VMEM)
    return pl.pallas_call(
        functools.partial(kernel, states, members, slots),
        out_shape=pltpu.VMEM((blocks, cols), jnp.float32),
        in_specs=[any_space] * 7,
        out_specs=vmem,
        scratch_shapes=[
            pltpu.VMEM(nbr_block.shape, jnp.int32),
            pltpu.VMEM(taper_index.shape, jnp.int32),
            pltpu.SMEM(pair_count.shape, jnp.int32),
            pltpu.VMEM((2, blocks, LANES), jnp.int32),
            pltpu.VMEM((3, blocks, LANES), jnp.int32),
            pltpu.SMEM((3, blocks, LANES), jnp.int32),
            pltpu.VMEM(cells.shape, jnp.int32),
            pltpu.VMEM(values.shape, jnp.float32),
            dma((6,)),
            pltpu.VMEM((blocks, mem, width), jnp.bfloat16),
            pltpu.VMEM(tapers.shape, jnp.bfloat16),
            pltpu.VMEM((blocks, mem, width), jnp.bfloat16),
            pltpu.VMEM((blocks, mem, width), jnp.bfloat16),
            pltpu.VMEM((2, blocks, LANES), jnp.int32),
            pltpu.SMEM((2, blocks, LANES), jnp.int32),
            pltpu.VMEM((blocks, width), jnp.float32),
            pltpu.VMEM((2, blocks, width), jnp.float32),
            pltpu.VMEM((3 * rows, obs_cell.shape[0]), jnp.bfloat16),
            pltpu.VMEM((LANES, obs_cell.shape[0]), jnp.bfloat16),
            pltpu.VMEM((chunks, KT * 3 * blocks + 1, MC, width), jnp.float32),
            pltpu.VMEM((chunks, blocks, MC, width), jnp.bfloat16),
            pltpu.VMEM((2 * blocks, MC, width), jnp.bfloat16),
            pltpu.VMEM((chunks // 2, blocks, MC, width), jnp.float32),
            pltpu.VMEM((3, blocks, 8, width), jnp.float32),
            pltpu.VMEM((3, members, blocks, cols), jnp.float32),
            pltpu.VMEM((3, members, blocks, cols), jnp.float32),
            dma((2,)), dma((2,)), dma((2,)), dma, dma,
            dma((chunks,)), dma((chunks,)),
            dma((chunks,)), dma((chunks,)),
            dma((members,)), dma((members,)), dma,
            dma((2,)), dma((2,)),
            dma((members,)), dma((members,)),
            dma((3, members)), dma((3, members)),
            pltpu.SemaphoreType.REGULAR,
            pltpu.SemaphoreType.REGULAR,
        ],
        compiler_params=pltpu.CompilerParams(
            collective_id=0, has_side_effects=True, vmem_limit_bytes=66_000_000
        ),
    )(nbr_block, taper_index, pair_count, cells, values, anomalies, tapers) / jnp.float32(M - 1)


def solution(mesh):
    placed = (
        P("state", "member", None),
        P(),
        P("state", None),
        P("state", None),
        P("state"),
        P("state"),
        P("state"),
    )
    return jax.shard_map(
        functools.partial(on_device, mesh.shape["state"], mesh.shape["member"]),
        mesh=mesh, in_specs=placed, out_specs=P("state", "member"), check_vma=False,
    )
```
